32 devices in a mesh: dp: 8 (over z, core), seq: 4 (over y, x).
Axes of the slice: x: 2, y: 2, z: 4, core: 2. Of those that a mesh axis runs over, the one named last changes fastest.
Arguments:
- tokens: bfloat16 [1024, 4096], P(('dp', 'seq')), may hold values from -6 to 6
- modality: int32 [1024], P(('dp', 'seq')), may hold values from 0 to 1, as said below
- gate_weight: bfloat16 [4096, 14336], P(None, 'dp'), may hold values from -0.09375 to 0.09375
- up_weight: bfloat16 [4096, 14336], P(None, 'dp'), may hold values from -0.09375 to 0.09375
- down_weight: bfloat16 [14336, 4096], P('dp'), may hold values from -0.046875 to 0.046875
- out_grad: bfloat16 [768, 4096], P(('dp', 'seq')), may hold values from -1.5 to 1.5
Outputs:
- output: bfloat16 [768, 4096], P(('dp', 'seq'))
- in_grad: bfloat16 [768, 4096], P(('dp', 'seq'))
- gate_grad: bfloat16 [4096, 14336], P('seq', 'dp')
- up_grad: bfloat16 [4096, 14336], P('seq', 'dp')
- down_grad: bfloat16 [14336, 4096], P('dp', 'seq')
The draws below stay inside these ranges and needn't reach their ends.
Inputs may be any that keep to these rules, and one draw needn't show every extreme that they name: In each aligned block of 32 tokens (the tokens of one device) exactly 24 tokens have modality 1 (vision); all others have 0 (text).
All inputs are finite; a program needn't handle non-finite values.
Results may differ from the reference program's by a relative error of at most 0.014.
Values may be sent and summed in bfloat16 or wider, within the bound.
No kernel may reach another device: no remote copies, remote signals or barrier semaphores. Data moves between devices by JAX's collectives and lax.ppermute only.
A program may use at most 192 MiB of HBM per device.

```python
import jax
import jax.numpy as jnp
from jax import lax

D = 4096
FF = 14336
TOK_DEV = 32
VIS_DEV = 24
TOKENS = 1024
VISION = 768
N_DP = 8
N_SEQ = 4


def draw_modality(key, part):
    block_count = TOKENS // TOK_DEV
    block_keys = jax.random.split(key, block_count)

    def one_block(block_key):
        order = jax.random.permutation(block_key, TOK_DEV)
        return (order < VIS_DEV).astype(jnp.int32)
    return jax.vmap(one_block)(block_keys).reshape(TOKENS)


def levels(stream_key, dims, cuts, least, high):
    factor_of = 1.0
    for position, blocks in cuts:
        draws = jax.random.uniform(jax.random.fold_in(jax.random.fold_in(stream_key, 6), position), (blocks,), jnp.float32, least / len(cuts), high / len(cuts))
        factor_of = factor_of * jnp.repeat(jnp.exp(draws), dims[position] // blocks).reshape((-1,) + (1,) * (len(dims) - 1 - position))
    return factor_of


def scatter_about(key, extent, width, most, pieces=(), held_as=jnp.bfloat16):
    values = width * jax.random.normal(key, extent, jnp.float32)
    if pieces:
        values = values * levels(key, extent, pieces, -0.22, 0.18)
    return jnp.clip(values, -most, most).astype(held_as)


def setup_inputs(seed: int = 0) -> dict:
    arg_keys = jax.random.split(jax.random.key(seed), 7)
    tokens = scatter_about(arg_keys[0], (TOKENS, D), 1.0, 6.0, ((0, 32),))
    modality = draw_modality(jax.random.fold_in(arg_keys[6], 71), 0)
    gate_weight = scatter_about(arg_keys[2], (D, FF), D ** -0.5, 0.09375, ((1, 8),))
    up_weight = scatter_about(arg_keys[3], (D, FF), D ** -0.5, 0.09375, ((1, 8),))
    down_weight = scatter_about(arg_keys[4], (FF, D), FF ** -0.5, 0.046875, ((0, 8),))
    out_grad = scatter_about(arg_keys[5], (VISION, D), 0.25, 1.5, ((0, 32),))
    return dict(tokens=tokens, modality=modality, gate_weight=gate_weight, up_weight=up_weight, down_weight=down_weight, out_grad=out_grad)


def silu_parts(gate_proj):
    sigmoid_value = jax.nn.sigmoid(gate_proj)
    return gate_proj * sigmoid_value, sigmoid_value * (1.0 + gate_proj * (1.0 - sigmoid_value))


def rounded(partial_sum):
    narrow = lax.optimization_barrier(partial_sum.astype(jnp.bfloat16))
    return narrow.astype(jnp.float32)


def by_group(matrix, group):
    blocks = matrix.reshape(N_DP, N_SEQ, VIS_DEV, matrix.shape[1])
    return blocks[:, group].reshape(N_DP * VIS_DEV, matrix.shape[1])


def reference(tokens, modality, gate_weight, up_weight, down_weight, out_grad):
    where_vision = jnp.nonzero(modality == 1, size=VISION)[0].astype(jnp.int32)
    picked = tokens[where_vision]
    gate_proj = jnp.dot(picked, gate_weight, preferred_element_type=jnp.float32)
    up_proj = jnp.dot(picked, up_weight, preferred_element_type=jnp.float32)
    active, slope = silu_parts(gate_proj)
    hidden = (active * up_proj).astype(jnp.bfloat16)
    output = jnp.dot(hidden, down_weight, preferred_element_type=jnp.float32).astype(jnp.bfloat16)
    back_hidden = jnp.dot(out_grad, down_weight.T, preferred_element_type=jnp.float32)
    gate_back = (back_hidden * up_proj * slope).astype(jnp.bfloat16)
    up_back = (back_hidden * active).astype(jnp.bfloat16)
    in_grad = (jnp.dot(gate_back, gate_weight.T, preferred_element_type=jnp.float32)
               + jnp.dot(up_back, up_weight.T, preferred_element_type=jnp.float32)).astype(jnp.bfloat16)
    gate_total = jnp.zeros((D, FF), jnp.float32)
    up_total = jnp.zeros((D, FF), jnp.float32)
    down_total = jnp.zeros((FF, D), jnp.float32)
    for group in range(N_SEQ):
        group_in = by_group(picked, group)
        gate_total = gate_total + rounded(jnp.dot(group_in.T, by_group(gate_back, group), preferred_element_type=jnp.float32))
        up_total = up_total + rounded(jnp.dot(group_in.T, by_group(up_back, group), preferred_element_type=jnp.float32))
        down_total = down_total + rounded(jnp.dot(by_group(hidden, group).T, by_group(out_grad, group), preferred_element_type=jnp.float32))
    return (output, in_grad, gate_total.astype(jnp.bfloat16), up_total.astype(jnp.bfloat16), down_total.astype(jnp.bfloat16))
```

```python
import functools

import jax
import jax.numpy as jnp
from jax import lax
from jax.experimental import pallas as pl
from jax.experimental.pallas import tpu as pltpu
from jax.sharding import PartitionSpec as P

BF = jnp.bfloat16
F32 = jnp.float32
CORES = 2


def tile_of(extent, options):
    for option in options:
        if extent % option == 0:
            return option
    return extent


def cost(flops, nbytes):
    return pl.CostEstimate(flops=flops, bytes_accessed=nbytes, transcendentals=0)


def shape(dims, dtype=BF):
    return jax.ShapeDtypeStruct(dims, dtype)


def nt_dot(left, right):
    return lax.dot_general(left, right, (((1,), (1,)), ((), ())), preferred_element_type=F32)


def nn_dot(left, right):
    return jnp.dot(left, right, preferred_element_type=F32)


def pick_kernel(flag_ref, tokens_ref, cot_ref, out_ref):
    rows, width = cot_ref.shape
    count = tokens_ref.shape[0]
    flags = (flag_ref[...] == 1).astype(F32)
    before = lax.broadcasted_iota(jnp.int32, (count, count), 0)
    after = lax.broadcasted_iota(jnp.int32, (count, count), 1)
    ranks = nn_dot(flags, (before <= after).astype(F32))
    slots = lax.broadcasted_iota(jnp.int32, (rows, count), 0).astype(F32) + 1.0
    chosen = (jnp.broadcast_to(ranks, (rows, count)) == slots) & (
        jnp.broadcast_to(flags, (rows, count)) == 1.0
    )
    out_ref[:, :width] = nn_dot(chosen.astype(BF), tokens_ref[...]).astype(BF)
    out_ref[:, width:] = cot_ref[...]


def pick(modality, tokens, out_grad):
    rows, width = out_grad.shape
    return pl.pallas_call(
        pick_kernel,
        out_shape=shape((rows, 2 * width)),
        name="pick",
    )(modality.reshape(1, -1), tokens, out_grad)


def hidden_kernel(xa_ref, xb_ref, ca_ref, cb_ref, gate_ref, up_ref, down_ref,
                  hid_ref, gb_ref, ub_ref, x_ref, c_ref):
    half = xa_ref.shape[0]

    @pl.when(pl.program_id(0) == 0)
    def _():
        x_ref[:half] = xa_ref[...]
        x_ref[half:] = xb_ref[...]
        c_ref[:half] = ca_ref[...]
        c_ref[half:] = cb_ref[...]

    gate_proj = nn_dot(x_ref[...], gate_ref[...])
    up_proj = nn_dot(x_ref[...], up_ref[...])
    back = nt_dot(c_ref[...], down_ref[...])
    sig = jax.nn.sigmoid(gate_proj)
    active = gate_proj * sig
    slope = sig * (1.0 + gate_proj * (1.0 - sig))
    hid_ref[...] = (active * up_proj).astype(BF)
    gb_ref[...] = (back * up_proj * slope).astype(BF)
    ub_ref[...] = (back * active).astype(BF)


def hidden_of(own, other, gate, up, down):
    half, both = own.shape
    width, units = gate.shape
    rows = 2 * half
    tile = tile_of(units, (256, 128))
    out = shape((rows, units))
    return pl.pallas_call(
        hidden_kernel,
        grid=(units // tile,),
        in_specs=[
            pl.BlockSpec((half, width), lambda j: (0, 0)),
            pl.BlockSpec((half, width), lambda j: (0, 0)),
            pl.BlockSpec((half, width), lambda j: (0, 1)),
            pl.BlockSpec((half, width), lambda j: (0, 1)),
            pl.BlockSpec((width, tile), lambda j: (0, j)),
            pl.BlockSpec((width, tile), lambda j: (0, j)),
            pl.BlockSpec((tile, width), lambda j: (j, 0)),
        ],
        out_specs=[pl.BlockSpec((rows, tile), lambda j: (0, j))] * 3,
        out_shape=[out] * 3,
        scratch_shapes=[pltpu.VMEM((rows, width), BF)] * 2,
        cost_estimate=cost(6 * rows * width * units, 6 * width * units),
        name="hidden",
    )(own, other, own, other, gate, up, down)


def back_kernel(hid_ref, gb_ref, ub_ref, gate_ref, up_ref, down_ref, own_ref, other_ref):
    half = own_ref.shape[1]
    result = nn_dot(hid_ref[...], down_ref[...]).astype(BF)
    own_ref[0] = result[:half]
    other_ref[0] = result[half:]
    result = (nt_dot(gb_ref[...], gate_ref[...]) + nt_dot(ub_ref[...], up_ref[...])).astype(BF)
    own_ref[1] = result[:half]
    other_ref[1] = result[half:]


def back_of(hid, gb, ub, gate, up, down):
    rows, units = hid.shape
    width = gate.shape[0]
    half = rows // 2
    tile = tile_of(width, (512, 256, 128))
    return pl.pallas_call(
        back_kernel,
        grid=(width // tile,),
        in_specs=[pl.BlockSpec((rows, units), lambda j: (0, 0))] * 3
        + [
            pl.BlockSpec((tile, units), lambda j: (j, 0)),
            pl.BlockSpec((tile, units), lambda j: (j, 0)),
            pl.BlockSpec((units, tile), lambda j: (0, j)),
        ],
        out_specs=[pl.BlockSpec((2, half, tile), lambda j: (0, 0, j))] * 2,
        out_shape=[shape((2, half, width))] * 2,
        cost_estimate=cost(6 * rows * width * units, 6 * width * units),
        name="back",
    )(hid, gb, ub, gate, up, down)


def right_kernel(parts, *refs):
    slices, values, out_ref, turned, stacked = (
        refs[:parts], refs[parts:2 * parts], refs[2 * parts], refs[2 * parts + 1], refs[2 * parts + 2])
    rows = slices[0].shape[0]

    @pl.when(pl.program_id(0) == 0)
    def _():
        for p in range(parts):
            stacked_rows = slices[p][...]
            turned[:, p * rows:(p + 1) * rows] = stacked_rows.T

    for p in range(parts):
        stacked[p * rows:(p + 1) * rows] = values[p][...]
    out_ref[...] = nn_dot(turned[...], stacked[...]).astype(BF)


def left_kernel(parts, *refs):
    slices, values, out_ref, held, turned = (
        refs[:parts], refs[parts:2 * parts], refs[2 * parts], refs[2 * parts + 1], refs[2 * parts + 2])
    rows = slices[0].shape[0]

    @pl.when(pl.program_id(0) == 0)
    def _():
        for p in range(parts):
            held[p * rows:(p + 1) * rows] = slices[p][...]

    for p in range(parts):
        turned[:, p * rows:(p + 1) * rows] = values[p][...].T
    out_ref[...] = nn_dot(turned[...], held[...]).astype(BF)


def grad_of(slices, values, column, left):
    parts = len(values)
    rows, units = values[0].shape
    width = slices[0].shape[1] // 2
    total = parts * rows
    tile = tile_of(units, (256, 128))
    if left:
        kernel, out, spec = left_kernel, (units, width), pl.BlockSpec((tile, width), lambda j: (j, 0))
        scratch = [pltpu.VMEM((total, width), BF), pltpu.VMEM((tile, total), BF)]
    else:
        kernel, out, spec = right_kernel, (width, units), pl.BlockSpec((width, tile), lambda j: (0, j))
        scratch = [pltpu.VMEM((width, total), BF), pltpu.VMEM((total, tile), BF)]
    return pl.pallas_call(
        functools.partial(kernel, parts),
        grid=(units // tile,),
        in_specs=[pl.BlockSpec((rows, width), lambda j: (0, column))] * parts
        + [pl.BlockSpec((rows, tile), lambda j: (0, j))] * parts,
        out_specs=spec,
        out_shape=shape(out),
        scratch_shapes=scratch,
        cost_estimate=cost(2 * total * width * units, 2 * (total * units + width * units)),
        name="grad_left" if left else "grad_right",
    )(*slices, *values)


def on_device(tokens, modality, gate, up, down, out_grad):
    count, width = out_grad.shape
    groups = lax.axis_size("seq")
    ring = lax.axis_size("dp") // CORES
    me = lax.axis_index("seq")
    part = width // groups

    def shift(value, k):
        return lax.ppermute(value, "dp", [
            (z * CORES + c, (z + k) % ring * CORES + c) for z in range(ring) for c in range(CORES)])

    def swap(value):
        return lax.ppermute(value, "dp", [
            (z * CORES + c, z * CORES + 1 - c) for z in range(ring) for c in range(CORES)])

    def across(value, mask):
        return lax.ppermute(value, "seq", [(g, g ^ mask) for g in range(groups)])

    def gathered(block):
        own = jnp.concatenate([block] + [shift(block, k) for k in range(1, ring)], axis=0)
        return own, swap(own)

    def cut(own, other, group):
        def columns(matrix, start):
            return lax.dynamic_slice_in_dim(matrix, start + group * part, part, axis=1)

        return jnp.concatenate([
            jnp.concatenate([columns(m, 0), columns(m, width)], axis=1) for m in (own, other)
        ], axis=0)

    near = [m for m in range(1, groups) if m & (m - 1) == 0]
    far = [m for m in range(1, groups) if m & (m - 1) != 0]

    block = pick(modality, tokens, out_grad)
    own, other = gathered(block)
    far_pairs = [gathered(across(block, m)) for m in far]
    near_slices = [across(cut(own, other, me ^ m), m) for m in near]
    hid, gb, ub = hidden_of(own, other, gate, up, down)
    near_hid = [across(hid, m) for m in near]
    near_gb = [across(gb, m) for m in near]
    near_ub = [across(ub, m) for m in near]

    mine, theirs = back_of(hid, gb, ub, gate, up, down)
    far_values = [hidden_of(a, b, gate, up, down) for a, b in far_pairs]

    summed = (mine.astype(F32) + swap(theirs).astype(F32)).astype(BF)
    pieces = summed.reshape(2, ring, count, width)
    total = pieces[:, 0].astype(F32)
    for k in range(1, ring):
        total = total + shift(pieces[:, k], -k).astype(F32)
    total = total.astype(BF)

    slices = [cut(own, other, me)] + near_slices + [cut(a, b, me) for a, b in far_pairs]
    down_grad = grad_of(slices, [hid] + near_hid + [v[0] for v in far_values], 1, True)
    gate_grad = grad_of(slices, [gb] + near_gb + [v[1] for v in far_values], 0, False)
    up_grad = grad_of(slices, [ub] + near_ub + [v[2] for v in far_values], 0, False)
    return total[0], total[1], gate_grad, up_grad, down_grad


def solution(mesh):
    rows = P(("dp", "seq"), None)
    return jax.shard_map(
        on_device,
        mesh=mesh,
        in_specs=(rows, P(("dp", "seq")), P(None, "dp"), P(None, "dp"), P("dp", None), rows),
        out_specs=(rows, rows, P("seq", "dp"), P("seq", "dp"), P("dp", "seq")),
        check_vma=False,
    )
```

```python
import jax
import jax.numpy as jnp
from jax import lax
from jax.experimental import pallas as pl
from jax.experimental.pallas import tpu as pltpu
from jax.sharding import PartitionSpec as P


BF = jnp.bfloat16
F32 = jnp.float32
CORES = 2
MIB = 1 << 20


ANY = pl.BlockSpec(memory_space=pl.ANY)
VMEM = pl.BlockSpec(memory_space=pltpu.VMEM)


def tile_of(extent, options):
    for option in options:
        if extent % option == 0:
            return option
    return extent


def cost(flops, nbytes):
    return pl.CostEstimate(flops=flops, bytes_accessed=nbytes, transcendentals=0)


def shape(dims, dtype=BF):
    return jax.ShapeDtypeStruct(dims, dtype)


def grant(*arrays):
    total = sum(2 * r * c if d == BF else 4 * r * c for r, c, d in arrays)
    return pltpu.CompilerParams(vmem_limit_bytes=min(total + 6 * MIB, 60 * MIB))


def nt_dot(left, right):
    return lax.dot_general(left, right, (((1,), (1,)), ((), ())), preferred_element_type=F32)


def nn_dot(left, right):
    return jnp.dot(left, right, preferred_element_type=F32)


def pick_kernel(flag_ref, tokens_ref, out_ref):
    rows = out_ref.shape[0]
    count = tokens_ref.shape[0]
    flags = (flag_ref[...] == 1).astype(F32)
    before = lax.broadcasted_iota(jnp.int32, (count, count), 0)
    after = lax.broadcasted_iota(jnp.int32, (count, count), 1)
    ranks = nn_dot(flags, (before <= after).astype(F32))
    slots = lax.broadcasted_iota(jnp.int32, (rows, count), 0).astype(F32) + 1.0
    chosen = (jnp.broadcast_to(ranks, (rows, count)) == slots) & (
        jnp.broadcast_to(flags, (rows, count)) == 1.0
    )
    out_ref[...] = nn_dot(chosen.astype(BF), tokens_ref[...]).astype(BF)


def pick(modality, tokens, rows):
    return pl.pallas_call(
        pick_kernel,
        out_shape=shape((rows, tokens.shape[1])),
        name="pick",
    )(modality.reshape(1, -1), tokens)


def enter_kernel(tile, xa_ref, xb_ref, gate_hbm, up_hbm, hid_ref, active_ref, turn_ref,
                 x_ref, gate_ref, up_ref, sems):
    half = xa_ref.shape[0]
    tiles = gate_ref.shape[0]

    def copies(j):
        column = pl.ds(pl.multiple_of(j * tile, tile), tile)
        return (
            pltpu.make_async_copy(gate_hbm.at[:, column], gate_ref.at[j], sems.at[0, j]),
            pltpu.make_async_copy(up_hbm.at[:, column], up_ref.at[j], sems.at[1, j]),
        )

    for j in range(tiles):
        for copy in copies(j):
            copy.start()
    x_ref[:half] = xa_ref[...]
    x_ref[half:] = xb_ref[...]

    @pl.loop(0, tiles)
    def _(j):
        column = pl.ds(pl.multiple_of(j * tile, tile), tile)
        for copy in copies(j):
            copy.wait()
        gate_proj = nn_dot(x_ref[...], gate_ref[j])
        up_proj = nn_dot(x_ref[...], up_ref[j])
        sig = jax.nn.sigmoid(gate_proj)
        active = gate_proj * sig
        hid_ref[:, column] = (active * up_proj).astype(BF)
        active_ref[:, column] = active
        turn_ref[:, column] = up_proj * (sig * (1.0 + gate_proj * (1.0 - sig)))


def enter(own, other, gate, up):
    half, width = own.shape
    units = gate.shape[1]
    rows = 2 * half
    tile = tile_of(units, (256, 128))
    tiles = units // tile
    return pl.pallas_call(
        lambda *refs: enter_kernel(tile, *refs),
        in_specs=[VMEM, VMEM, ANY, ANY],
        out_specs=[VMEM] * 3,
        out_shape=[shape((rows, units)), shape((rows, units), F32), shape((rows, units), F32)],
        scratch_shapes=[
            pltpu.VMEM((rows, width), BF),
            pltpu.VMEM((tiles, width, tile), BF),
            pltpu.VMEM((tiles, width, tile), BF),
            pltpu.SemaphoreType.DMA((2, tiles)),
        ],
        compiler_params=grant((2 * width, units, BF), (2 * rows, width, BF),
                              (rows, units, BF), (2 * rows, units, F32)),
        cost_estimate=cost(4 * rows * width * units, 4 * width * units),
        name="enter",
    )(own, other, gate, up)


def turn_kernel(tile, step, ca_ref, cb_ref, down_hbm, hid_ref, active_ref, factor_ref,
                gb_ref, ub_ref, own_ref, other_ref, c_ref, down_ref, sems):
    half = ca_ref.shape[0]
    units, width = down_ref.shape
    tiles = units // tile

    def copy(j):
        row = pl.ds(pl.multiple_of(j * tile, tile), tile)
        return pltpu.make_async_copy(down_hbm.at[row, :], down_ref.at[row, :], sems.at[j])

    for j in range(tiles):
        copy(j).start()
    c_ref[:half] = ca_ref[...]
    c_ref[half:] = cb_ref[...]

    @pl.loop(0, tiles)
    def _(j):
        span = pl.ds(pl.multiple_of(j * tile, tile), tile)
        copy(j).wait()
        back = nt_dot(c_ref[...], down_ref[span, :])
        gb_ref[:, span] = (back * factor_ref[:, span]).astype(BF)
        ub_ref[:, span] = (back * active_ref[:, span]).astype(BF)

    @pl.loop(0, width // step)
    def _(j):
        span = pl.ds(pl.multiple_of(j * step, step), step)
        result = nn_dot(hid_ref[...], down_ref[:, span]).astype(BF)
        own_ref[0, :, span] = result[:half]
        other_ref[0, :, span] = result[half:]


def turn(own, other, down, hid, active, factor):
    half, width = own.shape
    units = down.shape[0]
    rows = 2 * half
    tile = tile_of(units, (256, 128))
    step = tile_of(width, (512, 256, 128))
    return pl.pallas_call(
        lambda *refs: turn_kernel(tile, step, *refs),
        grid=(1,),
        in_specs=[VMEM, VMEM, ANY, VMEM, VMEM, VMEM],
        out_specs=[VMEM, VMEM] + [pl.BlockSpec((1, half, width), lambda i: (0, 0, 0))] * 2,
        out_shape=[shape((rows, units))] * 2 + [shape((2, half, width))] * 2,
        scratch_shapes=[
            pltpu.VMEM((rows, width), BF),
            pltpu.VMEM((units, width), BF),
            pltpu.SemaphoreType.DMA((units // tile,)),
        ],
        compiler_params=grant((width, units, BF), (4 * rows, width, BF),
                              (4 * rows, units, BF), (2 * rows, units, F32)),
        cost_estimate=cost(4 * rows * width * units, 2 * width * units),
        name="turn",
    )(own, other, down, hid, active, factor)


def leave_kernel(step, gb_ref, ub_ref, gate_hbm, up_hbm, own_in, other_in, own_ref, other_ref,
                 gate_ref, up_ref, sems):
    half = own_ref.shape[1]
    steps = gate_ref.shape[0] // step

    def copies(j):
        row = pl.ds(pl.multiple_of(j * step, step), step)
        return (
            pltpu.make_async_copy(gate_hbm.at[row, :], gate_ref.at[row, :], sems.at[0, j]),
            pltpu.make_async_copy(up_hbm.at[row, :], up_ref.at[row, :], sems.at[1, j]),
        )

    for j in range(steps):
        for copy in copies(j):
            copy.start()

    @pl.loop(0, steps)
    def _(j):
        span = pl.ds(pl.multiple_of(j * step, step), step)
        for copy in copies(j):
            copy.wait()
        result = nt_dot(gb_ref[...], gate_ref[span, :]) + nt_dot(ub_ref[...], up_ref[span, :])
        result = result.astype(BF)
        own_ref[0, :, span] = result[:half]
        other_ref[0, :, span] = result[half:]


def leave(gb, ub, gate, up, own, other):
    rows, units = gb.shape
    half, width = own.shape[1:]
    step = tile_of(width, (512, 256, 128))
    return pl.pallas_call(
        lambda *refs: leave_kernel(step, *refs),
        grid=(1,),
        in_specs=[VMEM, VMEM, ANY, ANY, ANY, ANY],
        out_specs=[pl.BlockSpec((1, half, width), lambda i: (1, 0, 0))] * 2,
        out_shape=[shape((2, half, width))] * 2,
        scratch_shapes=[
            pltpu.VMEM((width, units), BF),
            pltpu.VMEM((width, units), BF),
            pltpu.SemaphoreType.DMA((2, width // step)),
        ],
        input_output_aliases={4: 0, 5: 1},
        compiler_params=grant((2 * width, units, BF), (2 * rows, width, BF), (2 * rows, units, BF)),
        cost_estimate=cost(4 * rows * width * units, 4 * width * units),
        name="leave",
    )(gb, ub, gate, up, own, other)


def rows_dot(left, right):
    left, right = jnp.concatenate(left, axis=0), jnp.concatenate(right, axis=0)
    return lax.dot_general(
        left, right, (((0,), (0,)), ((), ())), preferred_element_type=F32
    ).astype(BF)


def on_device(tokens, modality, gate, up, down, out_grad):
    count, width = out_grad.shape
    groups = lax.axis_size("seq")
    ring = lax.axis_size("dp") // CORES
    me = lax.axis_index("seq")
    part = width // groups

    def shift(value, k):
        return lax.ppermute(value, "dp", [
            (z * CORES + c, (z + k) % ring * CORES + c) for z in range(ring) for c in range(CORES)])

    def swap(value):
        return lax.ppermute(value, "dp", [
            (z * CORES + c, z * CORES + 1 - c) for z in range(ring) for c in range(CORES)])

    def across(value, mask):
        return lax.ppermute(value, "seq", [(g, g ^ mask) for g in range(groups)])

    def gathered(block):
        return jnp.concatenate([block] + [shift(block, k) for k in range(1, ring)], axis=0)

    def cut(matrix, group):
        return lax.dynamic_slice_in_dim(matrix, group * part, part, axis=1)

    def slices_of(own):
        half = own.shape[0]
        far = [across(cut(own, me ^ m), m) for m in range(1, groups)]
        got = jnp.concatenate(far, axis=0)
        mate = swap(got)
        pairs = []
        for m in range(1, groups):
            pairs += [got[(m - 1) * half:m * half], mate[(m - 1) * half:m * half]]
        return pairs

    def spread(value, low):
        held = [value]
        for m in range(1, groups):
            bit = m & -m if low else 1 << (m.bit_length() - 1)
            held.append(across(held[m ^ bit], bit))
        return held

    block = pick(modality, tokens, count)
    tok = gathered(block)
    tok_mate = swap(tok)
    cot = gathered(out_grad)
    cot_mate = swap(cot)
    tok_far = slices_of(tok)
    hid, active, factor = enter(tok, tok_mate, gate, up)
    all_hid = spread(hid, True)
    cot_far = slices_of(cot)
    gb, ub, own, other = turn(cot, cot_mate, down, hid, active, factor)
    all_gb = spread(gb, True)
    all_ub = spread(ub, False)
    own, other = leave(gb, ub, gate, up, own, other)

    mate = swap(other)
    pieces = (own.astype(F32) + mate.astype(F32)).astype(BF).reshape(2, ring, count, width)
    total = pieces[:, 0].astype(F32)
    for k in range(1, ring):
        total = total + shift(pieces[:, k], -k).astype(F32)
    total = total.astype(BF)

    tok_all = [cut(tok, me), cut(tok_mate, me)] + tok_far
    cot_all = [cut(cot, me), cut(cot_mate, me)] + cot_far
    down_grad = rows_dot(all_hid, cot_all)
    gate_grad = rows_dot(tok_all, all_gb)
    up_grad = rows_dot(tok_all, all_ub)
    return total[0], total[1], gate_grad, up_grad, down_grad


def solution(mesh):
    rows = P(("dp", "seq"), None)
    return jax.shard_map(
        on_device,
        mesh=mesh,
        in_specs=(rows, P(("dp", "seq")), P(None, "dp"), P(None, "dp"), P("dp", None), rows),
        out_specs=(rows, rows, P("seq", "dp"), P("seq", "dp"), P("dp", "seq")),
        check_vma=False,
    )
```

```python
import jax
import jax.numpy as jnp
from jax import lax
from jax.experimental import pallas as pl
from jax.experimental.pallas import tpu as pltpu
from jax.sharding import PartitionSpec as P


BF = jnp.bfloat16
F32 = jnp.float32
CORES = 2
MIB = 1 << 20


ANY = pl.BlockSpec(memory_space=pl.ANY)
VMEM = pl.BlockSpec(memory_space=pltpu.VMEM)


def tile_of(extent, options):
    for option in options:
        if extent % option == 0:
            return option
    return extent


def cost(flops, nbytes):
    return pl.CostEstimate(flops=flops, bytes_accessed=nbytes, transcendentals=0)


def shape(dims, dtype=BF):
    return jax.ShapeDtypeStruct(dims, dtype)


def grant(*arrays):
    total = sum(2 * r * c if d == BF else 4 * r * c for r, c, d in arrays)
    return pltpu.CompilerParams(vmem_limit_bytes=min(total + 6 * MIB, 60 * MIB))


def nt_dot(left, right):
    return lax.dot_general(left, right, (((1,), (1,)), ((), ())), preferred_element_type=F32)


def nn_dot(left, right):
    return jnp.dot(left, right, preferred_element_type=F32)


def pick_kernel(flag_ref, tokens_ref, out_ref):
    rows = out_ref.shape[0]
    count = tokens_ref.shape[0]
    flags = (flag_ref[...] == 1).astype(F32)
    before = lax.broadcasted_iota(jnp.int32, (count, count), 0)
    after = lax.broadcasted_iota(jnp.int32, (count, count), 1)
    ranks = nn_dot(flags, (before <= after).astype(F32))
    slots = lax.broadcasted_iota(jnp.int32, (rows, count), 0).astype(F32) + 1.0
    chosen = (jnp.broadcast_to(ranks, (rows, count)) == slots) & (
        jnp.broadcast_to(flags, (rows, count)) == 1.0
    )
    out_ref[...] = nn_dot(chosen.astype(BF), tokens_ref[...]).astype(BF)


def pick(modality, tokens, rows):
    return pl.pallas_call(
        pick_kernel,
        out_shape=shape((rows, tokens.shape[1])),
        name="pick",
    )(modality.reshape(1, -1), tokens)


def enter_kernel(tile, xa_ref, xb_ref, gate_hbm, up_hbm, hid_ref, active_ref, turn_ref,
                 x_ref, gate_ref, up_ref, sems):
    half = xa_ref.shape[0]
    tiles = gate_ref.shape[0]

    def copies(j):
        column = pl.ds(pl.multiple_of(j * tile, tile), tile)
        return (
            pltpu.make_async_copy(gate_hbm.at[:, column], gate_ref.at[j], sems.at[0, j]),
            pltpu.make_async_copy(up_hbm.at[:, column], up_ref.at[j], sems.at[1, j]),
        )

    for j in range(tiles):
        for copy in copies(j):
            copy.start()
    x_ref[:half] = xa_ref[...]
    x_ref[half:] = xb_ref[...]

    @pl.loop(0, tiles)
    def _(j):
        column = pl.ds(pl.multiple_of(j * tile, tile), tile)
        for copy in copies(j):
            copy.wait()
        gate_proj = nn_dot(x_ref[...], gate_ref[j])
        up_proj = nn_dot(x_ref[...], up_ref[j])
        sig = jax.nn.sigmoid(gate_proj)
        active = gate_proj * sig
        hid_ref[:, column] = (active * up_proj).astype(BF)
        active_ref[:, column] = active
        turn_ref[:, column] = up_proj * (sig * (1.0 + gate_proj * (1.0 - sig)))


def enter(own, other, gate, up):
    half, width = own.shape
    units = gate.shape[1]
    rows = 2 * half
    tile = tile_of(units, (256, 128))
    tiles = units // tile
    return pl.pallas_call(
        lambda *refs: enter_kernel(tile, *refs),
        in_specs=[VMEM, VMEM, ANY, ANY],
        out_specs=[VMEM] * 3,
        out_shape=[shape((rows, units)), shape((rows, units), F32), shape((rows, units), F32)],
        scratch_shapes=[
            pltpu.VMEM((rows, width), BF),
            pltpu.VMEM((tiles, width, tile), BF),
            pltpu.VMEM((tiles, width, tile), BF),
            pltpu.SemaphoreType.DMA((2, tiles)),
        ],
        compiler_params=grant((2 * width, units, BF), (2 * rows, width, BF),
                              (rows, units, BF), (2 * rows, units, F32)),
        cost_estimate=cost(4 * rows * width * units, 4 * width * units),
        name="enter",
    )(own, other, gate, up)


def turn_kernel(tile, step, ca_ref, cb_ref, down_hbm, hid_ref, active_ref, factor_ref,
                gb_ref, ub_ref, own_ref, other_ref, c_ref, down_ref, sems):
    half = ca_ref.shape[0]
    units, width = down_ref.shape
    tiles = units // tile

    def copy(j):
        row = pl.ds(pl.multiple_of(j * tile, tile), tile)
        return pltpu.make_async_copy(down_hbm.at[row, :], down_ref.at[row, :], sems.at[j])

    for j in range(tiles):
        copy(j).start()
    c_ref[:half] = ca_ref[...]
    c_ref[half:] = cb_ref[...]

    @pl.loop(0, tiles)
    def _(j):
        span = pl.ds(pl.multiple_of(j * tile, tile), tile)
        copy(j).wait()
        back = nt_dot(c_ref[...], down_ref[span, :])
        gb_ref[:, span] = (back * factor_ref[:, span]).astype(BF)
        ub_ref[:, span] = (back * active_ref[:, span]).astype(BF)

    @pl.loop(0, width // step)
    def _(j):
        span = pl.ds(pl.multiple_of(j * step, step), step)
        result = nn_dot(hid_ref[...], down_ref[:, span]).astype(BF)
        own_ref[0, :, span] = result[:half]
        other_ref[0, :, span] = result[half:]


def turn(own, other, down, hid, active, factor):
    half, width = own.shape
    units = down.shape[0]
    rows = 2 * half
    tile = tile_of(units, (256, 128))
    step = tile_of(width, (512, 256, 128))
    return pl.pallas_call(
        lambda *refs: turn_kernel(tile, step, *refs),
        grid=(1,),
        in_specs=[VMEM, VMEM, ANY, VMEM, VMEM, VMEM],
        out_specs=[VMEM, VMEM] + [pl.BlockSpec((1, half, width), lambda i: (0, 0, 0))] * 2,
        out_shape=[shape((rows, units))] * 2 + [shape((2, half, width))] * 2,
        scratch_shapes=[
            pltpu.VMEM((rows, width), BF),
            pltpu.VMEM((units, width), BF),
            pltpu.SemaphoreType.DMA((units // tile,)),
        ],
        compiler_params=grant((width, units, BF), (4 * rows, width, BF),
                              (4 * rows, units, BF), (2 * rows, units, F32)),
        cost_estimate=cost(4 * rows * width * units, 2 * width * units),
        name="turn",
    )(own, other, down, hid, active, factor)


def leave_kernel(step, gb_ref, ub_ref, gate_hbm, up_hbm, own_in, other_in, own_ref, other_ref,
                 gate_ref, up_ref, sems):
    half = own_ref.shape[1]
    steps = gate_ref.shape[0] // step

    def copies(j):
        row = pl.ds(pl.multiple_of(j * step, step), step)
        return (
            pltpu.make_async_copy(gate_hbm.at[row, :], gate_ref.at[row, :], sems.at[0, j]),
            pltpu.make_async_copy(up_hbm.at[row, :], up_ref.at[row, :], sems.at[1, j]),
        )

    for j in range(steps):
        for copy in copies(j):
            copy.start()

    @pl.loop(0, steps)
    def _(j):
        span = pl.ds(pl.multiple_of(j * step, step), step)
        for copy in copies(j):
            copy.wait()
        result = nt_dot(gb_ref[...], gate_ref[span, :]) + nt_dot(ub_ref[...], up_ref[span, :])
        result = result.astype(BF)
        own_ref[0, :, span] = result[:half]
        other_ref[0, :, span] = result[half:]


def leave(gb, ub, gate, up, own, other):
    rows, units = gb.shape
    half, width = own.shape[1:]
    step = tile_of(width, (512, 256, 128))
    return pl.pallas_call(
        lambda *refs: leave_kernel(step, *refs),
        grid=(1,),
        in_specs=[VMEM, VMEM, ANY, ANY, ANY, ANY],
        out_specs=[pl.BlockSpec((1, half, width), lambda i: (1, 0, 0))] * 2,
        out_shape=[shape((2, half, width))] * 2,
        scratch_shapes=[
            pltpu.VMEM((width, units), BF),
            pltpu.VMEM((width, units), BF),
            pltpu.SemaphoreType.DMA((2, width // step)),
        ],
        input_output_aliases={4: 0, 5: 1},
        compiler_params=grant((2 * width, units, BF), (2 * rows, width, BF), (2 * rows, units, BF)),
        cost_estimate=cost(4 * rows * width * units, 4 * width * units),
        name="leave",
    )(gb, ub, gate, up, own, other)


def rows_dot(left, right):
    left, right = jnp.concatenate(left, axis=0), jnp.concatenate(right, axis=0)
    return lax.dot_general(
        left, right, (((0,), (0,)), ((), ())), preferred_element_type=F32
    ).astype(BF)


def on_device(tokens, modality, gate, up, down, out_grad):
    count, width = out_grad.shape
    groups = lax.axis_size("seq")
    ring = lax.axis_size("dp") // CORES
    me = lax.axis_index("seq")
    part = width // groups

    def shift(value, k):
        return lax.ppermute(value, "dp", [
            (z * CORES + c, (z + k) % ring * CORES + c) for z in range(ring) for c in range(CORES)])

    def swap(value):
        return lax.ppermute(value, "dp", [
            (z * CORES + c, z * CORES + 1 - c) for z in range(ring) for c in range(CORES)])

    def across(value, mask):
        return lax.ppermute(value, "seq", [(g, g ^ mask) for g in range(groups)])

    def gathered(block):
        return jnp.concatenate([block] + [shift(block, k) for k in range(1, ring)], axis=0)

    def cut(matrix, group):
        return lax.dynamic_slice_in_dim(matrix, group * part, part, axis=1)

    def slices_of(own):
        half = own.shape[0]
        far = [across(cut(own, me ^ m), m) for m in range(1, groups)]
        got = jnp.concatenate(far, axis=0)
        mate = swap(got)
        pairs = []
        for m in range(1, groups):
            pairs += [got[(m - 1) * half:m * half], mate[(m - 1) * half:m * half]]
        return pairs

    def spread(value, way):
        held = [[value]]
        for m in range(1, groups):
            low, high = m & -m, 1 << (m.bit_length() - 1)
            if low == high:
                held.append([across(value, m)])
            elif way == "both":
                a = jnp.concatenate(held[m ^ low], axis=0)
                b = jnp.concatenate(held[m ^ high], axis=0)
                half = a.shape[0] // 2
                held.append([across(a[:half], low), across(b[half:], high)])
            else:
                bit = low if way == "low" else high
                held.append([across(held[m ^ bit][0], bit)])
        return sum(held, [])

    block = pick(modality, tokens, count)
    tok = gathered(block)
    tok_mate = swap(tok)
    cot = gathered(out_grad)
    cot_mate = swap(cot)
    tok_far = slices_of(tok)
    hid, active, factor = enter(tok, tok_mate, gate, up)
    all_hid = spread(hid, "both")
    cot_far = slices_of(cot)
    gb, ub, own, other = turn(cot, cot_mate, down, hid, active, factor)
    all_gb = spread(gb, "low")
    all_ub = spread(ub, "high")
    own, other = leave(gb, ub, gate, up, own, other)

    mate = swap(other)
    pieces = (own.astype(F32) + mate.astype(F32)).astype(BF).reshape(2, ring, count, width)
    total = pieces[:, 0].astype(F32)
    for k in range(1, ring):
        total = total + shift(pieces[:, k], -k).astype(F32)
    total = total.astype(BF)

    tok_all = [cut(tok, me), cut(tok_mate, me)] + tok_far
    cot_all = [cut(cot, me), cut(cot_mate, me)] + cot_far
    down_grad = rows_dot(all_hid, cot_all)
    gate_grad = rows_dot(tok_all, all_gb)
    up_grad = rows_dot(tok_all, all_ub)
    return total[0], total[1], gate_grad, up_grad, down_grad


def solution(mesh):
    rows = P(("dp", "seq"), None)
    return jax.shard_map(
        on_device,
        mesh=mesh,
        in_specs=(rows, P(("dp", "seq")), P(None, "dp"), P(None, "dp"), P("dp", None), rows),
        out_specs=(rows, rows, P("seq", "dp"), P("seq", "dp"), P("dp", "seq")),
        check_vma=False,
    )
```

```python
import jax
import jax.numpy as jnp
from jax import lax
from jax.experimental import pallas as pl
from jax.experimental.pallas import tpu as pltpu
from jax.sharding import PartitionSpec as P


BF = jnp.bfloat16
F32 = jnp.float32
CORES = 2
MIB = 1 << 20


ANY = pl.BlockSpec(memory_space=pl.ANY)
VMEM = pl.BlockSpec(memory_space=pltpu.VMEM)


def tile_of(extent, options):
    for option in options:
        if extent % option == 0:
            return option
    return extent


def cost(flops, nbytes):
    return pl.CostEstimate(flops=flops, bytes_accessed=nbytes, transcendentals=0)


def shape(dims, dtype=BF):
    return jax.ShapeDtypeStruct(dims, dtype)


def grant(*arrays):
    total = sum(2 * r * c if d == BF else 4 * r * c for r, c, d in arrays)
    return pltpu.CompilerParams(vmem_limit_bytes=min(total + 6 * MIB, 60 * MIB))


def nt_dot(left, right):
    return lax.dot_general(left, right, (((1,), (1,)), ((), ())), preferred_element_type=F32)


def nn_dot(left, right):
    return jnp.dot(left, right, preferred_element_type=F32)


def pick_kernel(flag_ref, tokens_ref, out_ref):
    rows = out_ref.shape[0]
    count = tokens_ref.shape[0]
    flags = (flag_ref[...] == 1).astype(F32)
    before = lax.broadcasted_iota(jnp.int32, (count, count), 0)
    after = lax.broadcasted_iota(jnp.int32, (count, count), 1)
    ranks = nn_dot(flags, (before <= after).astype(F32))
    slots = lax.broadcasted_iota(jnp.int32, (rows, count), 0).astype(F32) + 1.0
    chosen = (jnp.broadcast_to(ranks, (rows, count)) == slots) & (
        jnp.broadcast_to(flags, (rows, count)) == 1.0
    )
    out_ref[...] = nn_dot(chosen.astype(BF), tokens_ref[...]).astype(BF)


def pick(modality, tokens, rows):
    return pl.pallas_call(
        pick_kernel,
        out_shape=shape((rows, tokens.shape[1])),
        name="pick",
    )(modality.reshape(1, -1), tokens)


def enter_kernel(tile, xa_ref, xb_ref, gate_hbm, up_hbm, hid_ref, active_ref, turn_ref,
                 x_ref, gate_ref, up_ref, sems):
    half = xa_ref.shape[0]
    tiles = gate_ref.shape[0]

    def copies(j):
        column = pl.ds(pl.multiple_of(j * tile, tile), tile)
        return (
            pltpu.make_async_copy(gate_hbm.at[:, column], gate_ref.at[j], sems.at[0, j]),
            pltpu.make_async_copy(up_hbm.at[:, column], up_ref.at[j], sems.at[1, j]),
        )

    for j in range(tiles):
        for copy in copies(j):
            copy.start()
    x_ref[:half] = xa_ref[...]
    x_ref[half:] = xb_ref[...]

    @pl.loop(0, tiles)
    def _(j):
        column = pl.ds(pl.multiple_of(j * tile, tile), tile)
        for copy in copies(j):
            copy.wait()
        gate_proj = nn_dot(x_ref[...], gate_ref[j])
        up_proj = nn_dot(x_ref[...], up_ref[j])
        sig = jax.nn.sigmoid(gate_proj)
        active = gate_proj * sig
        hid_ref[:, column] = (active * up_proj).astype(BF)
        active_ref[:, column] = active
        turn_ref[:, column] = up_proj * (sig * (1.0 + gate_proj * (1.0 - sig)))


def enter(own, other, gate, up):
    half, width = own.shape
    units = gate.shape[1]
    rows = 2 * half
    tile = tile_of(units, (256, 128))
    tiles = units // tile
    return pl.pallas_call(
        lambda *refs: enter_kernel(tile, *refs),
        in_specs=[VMEM, VMEM, ANY, ANY],
        out_specs=[VMEM] * 3,
        out_shape=[shape((rows, units)), shape((rows, units), F32), shape((rows, units), F32)],
        scratch_shapes=[
            pltpu.VMEM((rows, width), BF),
            pltpu.VMEM((tiles, width, tile), BF),
            pltpu.VMEM((tiles, width, tile), BF),
            pltpu.SemaphoreType.DMA((2, tiles)),
        ],
        compiler_params=grant((2 * width, units, BF), (2 * rows, width, BF),
                              (rows, units, BF), (2 * rows, units, F32)),
        cost_estimate=cost(4 * rows * width * units, 4 * width * units),
        name="enter",
    )(own, other, gate, up)


def turn_kernel(tile, step, ca_ref, cb_ref, down_hbm, hid_ref, active_ref, factor_ref,
                gb_ref, ub_ref, own_ref, other_ref, c_ref, down_ref, sems):
    half = ca_ref.shape[0]
    units, width = down_ref.shape
    tiles = units // tile

    def copy(j):
        row = pl.ds(pl.multiple_of(j * tile, tile), tile)
        return pltpu.make_async_copy(down_hbm.at[row, :], down_ref.at[row, :], sems.at[j])

    for j in range(tiles):
        copy(j).start()
    c_ref[:half] = ca_ref[...]
    c_ref[half:] = cb_ref[...]

    @pl.loop(0, tiles)
    def _(j):
        span = pl.ds(pl.multiple_of(j * tile, tile), tile)
        copy(j).wait()
        back = nt_dot(c_ref[...], down_ref[span, :])
        gb_ref[:, span] = (back * factor_ref[:, span]).astype(BF)
        ub_ref[:, span] = (back * active_ref[:, span]).astype(BF)

    @pl.loop(0, width // step)
    def _(j):
        span = pl.ds(pl.multiple_of(j * step, step), step)
        result = nn_dot(hid_ref[...], down_ref[:, span]).astype(BF)
        own_ref[0, :, span] = result[:half]
        other_ref[0, :, span] = result[half:]


def turn(own, other, down, hid, active, factor):
    half, width = own.shape
    units = down.shape[0]
    rows = 2 * half
    tile = tile_of(units, (256, 128))
    step = tile_of(width, (512, 256, 128))
    return pl.pallas_call(
        lambda *refs: turn_kernel(tile, step, *refs),
        grid=(1,),
        in_specs=[VMEM, VMEM, ANY, VMEM, VMEM, VMEM],
        out_specs=[VMEM, VMEM] + [pl.BlockSpec((1, half, width), lambda i: (0, 0, 0))] * 2,
        out_shape=[shape((rows, units))] * 2 + [shape((2, half, width))] * 2,
        scratch_shapes=[
            pltpu.VMEM((rows, width), BF),
            pltpu.VMEM((units, width), BF),
            pltpu.SemaphoreType.DMA((units // tile,)),
        ],
        compiler_params=grant((width, units, BF), (4 * rows, width, BF),
                              (4 * rows, units, BF), (2 * rows, units, F32)),
        cost_estimate=cost(4 * rows * width * units, 2 * width * units),
        name="turn",
    )(own, other, down, hid, active, factor)


def leave_kernel(step, gb_ref, ub_ref, gate_hbm, up_hbm, own_in, other_in, own_ref, other_ref,
                 gate_ref, up_ref, sems):
    half = own_ref.shape[1]
    steps = gate_ref.shape[0] // step

    def copies(j):
        row = pl.ds(pl.multiple_of(j * step, step), step)
        return (
            pltpu.make_async_copy(gate_hbm.at[row, :], gate_ref.at[row, :], sems.at[0, j]),
            pltpu.make_async_copy(up_hbm.at[row, :], up_ref.at[row, :], sems.at[1, j]),
        )

    for j in range(steps):
        for copy in copies(j):
            copy.start()

    @pl.loop(0, steps)
    def _(j):
        span = pl.ds(pl.multiple_of(j * step, step), step)
        for copy in copies(j):
            copy.wait()
        result = nt_dot(gb_ref[...], gate_ref[span, :]) + nt_dot(ub_ref[...], up_ref[span, :])
        result = result.astype(BF)
        own_ref[0, :, span] = result[:half]
        other_ref[0, :, span] = result[half:]


def leave(gb, ub, gate, up, own, other):
    rows, units = gb.shape
    half, width = own.shape[1:]
    step = tile_of(width, (512, 256, 128))
    return pl.pallas_call(
        lambda *refs: leave_kernel(step, *refs),
        grid=(1,),
        in_specs=[VMEM, VMEM, ANY, ANY, ANY, ANY],
        out_specs=[pl.BlockSpec((1, half, width), lambda i: (1, 0, 0))] * 2,
        out_shape=[shape((2, half, width))] * 2,
        scratch_shapes=[
            pltpu.VMEM((width, units), BF),
            pltpu.VMEM((width, units), BF),
            pltpu.SemaphoreType.DMA((2, width // step)),
        ],
        input_output_aliases={4: 0, 5: 1},
        compiler_params=grant((2 * width, units, BF), (2 * rows, width, BF), (2 * rows, units, BF)),
        cost_estimate=cost(4 * rows * width * units, 4 * width * units),
        name="leave",
    )(gb, ub, gate, up, own, other)


def rows_dot(left, right):
    return lax.dot_general(
        left, right, (((0,), (0,)), ((), ())), preferred_element_type=F32
    ).astype(BF)


def on_device(tokens, modality, gate, up, down, out_grad):
    count, width = out_grad.shape
    groups = lax.axis_size("seq")
    ring = lax.axis_size("dp") // CORES
    me = lax.axis_index("seq")
    part = width // groups

    def shift(value, k):
        return lax.ppermute(value, "dp", [
            (z * CORES + c, (z + k) % ring * CORES + c) for z in range(ring) for c in range(CORES)])

    def swap(value):
        return lax.ppermute(value, "dp", [
            (z * CORES + c, z * CORES + 1 - c) for z in range(ring) for c in range(CORES)])

    def across(value, mask):
        return lax.ppermute(value, "seq", [(g, g ^ mask) for g in range(groups)])

    def gathered(block):
        return jnp.concatenate([block] + [shift(block, k) for k in range(1, ring)], axis=0)

    def cut(matrix, group):
        return lax.dynamic_slice_in_dim(matrix, group * part, part, axis=1)

    def slices_of(tok_block, cot_block):
        def both(group):
            return jnp.concatenate([cut(tok_block, group), cut(cot_block, group)], axis=1)

        small = jnp.stack(
            [both(me)] + [across(both(me ^ m), m) for m in range(1, groups)])
        pieces = [small] + [shift(small, k) for k in range(1, ring)]
        own = jnp.stack(pieces, axis=1)
        mate = swap(own)
        both_cores = jnp.stack([own, mate], axis=1)
        return (both_cores[..., :part].reshape(-1, part), both_cores[..., part:].reshape(-1, part))

    def near(value):
        held = [[value]] + [None] * (groups - 1)
        for m in range(1, groups):
            if m & (m - 1) == 0:
                held[m] = [across(value, m)]
        return held

    def relay(held):
        half = held[0][0].shape[0] // 2
        held = list(held)
        for m in range(1, groups):
            low, high = m & -m, 1 << (m.bit_length() - 1)
            if low != high:
                a = jnp.concatenate(held[m ^ low], axis=0)
                b = jnp.concatenate(held[m ^ high], axis=0)
                held[m] = [across(a[:half], low), across(b[half:], high)]
        return held

    def after(values, others):
        leaves, tree = jax.tree.flatten(values)
        return jax.tree.unflatten(
            tree, lax.optimization_barrier((*leaves, *others))[:len(leaves)])

    def stack(held):
        return jnp.concatenate(sum(held, []), axis=0)

    block = pick(modality, tokens, count)
    tok = gathered(block)
    tok_mate = swap(tok)
    tok_all, cot_all = slices_of(block, out_grad)
    cot = gathered(out_grad)
    cot_mate = swap(cot)
    hid, active, factor = enter(tok, tok_mate, gate, up)
    all_hid = relay(near(hid))
    gb, ub, own, other = turn(cot, cot_mate, down, hid, active, factor)
    all_gb = near(gb)
    all_ub = near(ub)
    own, other = leave(gb, ub, gate, up, own, other)

    mate = swap(other)
    sums = (own.astype(F32) + mate.astype(F32)).astype(BF).reshape(2, ring, count, width)
    sums = [sums[:, k] for k in range(ring)]
    terms = [shift(sums[k], -k) for k in range(1, ring)]

    all_hid = after(all_hid, sums[1:])
    all_gb = relay(after(all_gb, sums[1:]))
    all_ub = relay(after(all_ub, sums[1:]))
    down_grad = rows_dot(stack(all_hid), cot_all)
    gate_grad = rows_dot(tok_all, stack(all_gb))
    up_grad = rows_dot(tok_all, stack(all_ub))
    terms = after(terms, [gate_grad])
    total = sums[0].astype(F32)
    for term in terms:
        total = total + term.astype(F32)
    total = total.astype(BF)
    return total[0], total[1], gate_grad, up_grad, down_grad


def solution(mesh):
    rows = P(("dp", "seq"), None)
    return jax.shard_map(
        on_device,
        mesh=mesh,
        in_specs=(rows, P(("dp", "seq")), P(None, "dp"), P(None, "dp"), P("dp", None), rows),
        out_specs=(rows, rows, P("seq", "dp"), P("seq", "dp"), P("dp", "seq")),
        check_vma=False,
    )
```

```python
import jax
import jax.numpy as jnp
from jax import lax
from jax.experimental import pallas as pl
from jax.experimental.pallas import tpu as pltpu
from jax.sharding import PartitionSpec as P


BF = jnp.bfloat16
F32 = jnp.float32
CORES = 2
MIB = 1 << 20


HBM = pl.BlockSpec(memory_space=pltpu.HBM)
VMEM = pl.BlockSpec(memory_space=pltpu.VMEM)


def tile_of(extent, options):
    for option in options:
        if extent % option == 0:
            return option
    return extent


def cost(flops, nbytes):
    return pl.CostEstimate(flops=flops, bytes_accessed=nbytes, transcendentals=0)


def shape(dims, dtype=BF):
    return jax.ShapeDtypeStruct(dims, dtype)


def grant(*arrays):
    total = sum(2 * r * c if d == BF else 4 * r * c for r, c, d in arrays)
    return pltpu.CompilerParams(vmem_limit_bytes=min(total + 6 * MIB, 60 * MIB))


def nt_dot(left, right):
    return lax.dot_general(left, right, (((1,), (1,)), ((), ())), preferred_element_type=F32)


def nn_dot(left, right):
    return jnp.dot(left, right, preferred_element_type=F32)


def pick_kernel(flag_ref, tokens_ref, out_ref):
    rows = out_ref.shape[0]
    count = tokens_ref.shape[0]
    flags = (flag_ref[...] == 1).astype(F32)
    before = lax.broadcasted_iota(jnp.int32, (count, count), 0)
    after = lax.broadcasted_iota(jnp.int32, (count, count), 1)
    ranks = nn_dot(flags, (before <= after).astype(F32))
    slots = lax.broadcasted_iota(jnp.int32, (rows, count), 0).astype(F32) + 1.0
    chosen = (jnp.broadcast_to(ranks, (rows, count)) == slots) & (
        jnp.broadcast_to(flags, (rows, count)) == 1.0
    )
    out_ref[...] = nn_dot(chosen.astype(BF), tokens_ref[...]).astype(BF)


def pick(modality, tokens, rows):
    return pl.pallas_call(
        pick_kernel,
        out_shape=shape((rows, tokens.shape[1])),
        compiler_params=grant(),
        name="pick",
    )(modality.reshape(1, -1), tokens)


def streamed(steps, depth, copies, body):
    depth = min(depth, steps)

    def start(j):
        for copy in copies(j, lax.rem(j, depth)):
            copy.start()

    for j in range(depth):
        start(jnp.int32(j))

    @pl.loop(0, steps)
    def _(j):
        slot = lax.rem(j, depth)
        for copy in copies(j, slot):
            copy.wait()
        body(j, slot)

        @pl.when(j + depth < steps)
        def _():
            start(j + depth)


DEPTH = 4


def enter_kernel(tile, xa_ref, xb_ref, gate_hbm, up_hbm, hid_ref, active_ref, turn_ref,
                 x_ref, gate_ref, up_ref, sems):
    half = xa_ref.shape[0]
    x_ref[:half] = xa_ref[...]
    x_ref[half:] = xb_ref[...]

    def copies(j, slot):
        column = pl.ds(pl.multiple_of(j * tile, tile), tile)
        return (
            pltpu.make_async_copy(gate_hbm.at[:, column], gate_ref.at[slot], sems.at[0, slot]),
            pltpu.make_async_copy(up_hbm.at[:, column], up_ref.at[slot], sems.at[1, slot]),
        )

    def body(j, slot):
        column = pl.ds(pl.multiple_of(j * tile, tile), tile)
        gate_proj = nn_dot(x_ref[...], gate_ref[slot])
        up_proj = nn_dot(x_ref[...], up_ref[slot])
        sig = jax.nn.sigmoid(gate_proj)
        active = gate_proj * sig
        hid_ref[:, column] = (active * up_proj).astype(BF)
        active_ref[:, column] = active
        turn_ref[:, column] = up_proj * (sig * (1.0 + gate_proj * (1.0 - sig)))

    streamed(gate_hbm.shape[1] // tile, gate_ref.shape[0], copies, body)


def enter(own, other, gate, up):
    half, width = own.shape
    units = gate.shape[1]
    rows = 2 * half
    tile = tile_of(units, (256, 128))
    depth = min(DEPTH, units // tile)
    return pl.pallas_call(
        lambda *refs: enter_kernel(tile, *refs),
        in_specs=[VMEM, VMEM, HBM, HBM],
        out_specs=[VMEM] * 3,
        out_shape=[shape((rows, units)), shape((rows, units), F32), shape((rows, units), F32)],
        scratch_shapes=[
            pltpu.VMEM((rows, width), BF),
            pltpu.VMEM((depth, width, tile), BF),
            pltpu.VMEM((depth, width, tile), BF),
            pltpu.SemaphoreType.DMA((2, depth)),
        ],
        compiler_params=grant((rows, width, BF), (2 * depth * tile, width, BF)),
        cost_estimate=cost(4 * rows * width * units, 4 * width * units),
        name="enter",
    )(own, other, gate, up)


def turn_kernel(tile, ca_ref, cb_ref, down_hbm, active_ref, factor_ref, gb_ref, ub_ref,
                c_ref, down_ref, sems):
    half = ca_ref.shape[0]
    c_ref[:half] = ca_ref[...]
    c_ref[half:] = cb_ref[...]

    def copies(j, slot):
        row = pl.ds(pl.multiple_of(j * tile, tile), tile)
        return (pltpu.make_async_copy(down_hbm.at[row, :], down_ref.at[slot], sems.at[slot]),)

    def body(j, slot):
        span = pl.ds(pl.multiple_of(j * tile, tile), tile)
        back = nt_dot(c_ref[...], down_ref[slot])
        gb_ref[:, span] = (back * factor_ref[:, span]).astype(BF)
        ub_ref[:, span] = (back * active_ref[:, span]).astype(BF)

    streamed(down_hbm.shape[0] // tile, down_ref.shape[0], copies, body)


def turn(own, other, down, active, factor):
    half, width = own.shape
    units = down.shape[0]
    rows = 2 * half
    tile = tile_of(units, (256, 128))
    depth = min(DEPTH, units // tile)
    return pl.pallas_call(
        lambda *refs: turn_kernel(tile, *refs),
        in_specs=[VMEM, VMEM, HBM, VMEM, VMEM],
        out_specs=[VMEM] * 2,
        out_shape=[shape((rows, units))] * 2,
        scratch_shapes=[
            pltpu.VMEM((rows, width), BF),
            pltpu.VMEM((depth, tile, width), BF),
            pltpu.SemaphoreType.DMA((depth,)),
        ],
        compiler_params=grant((rows, width, BF), (depth * tile, width, BF)),
        cost_estimate=cost(2 * rows * width * units, 2 * width * units),
        name="turn",
    )(own, other, down, active, factor)


def leave_kernel(step, hid_ref, gb_ref, ub_ref, gate_hbm, up_hbm, down_hbm, own_ref, other_ref,
                 gate_ref, up_ref, down_ref, sems):
    half = own_ref.shape[1]

    def copies(j, slot):
        span = pl.ds(pl.multiple_of(j * step, step), step)
        return (
            pltpu.make_async_copy(down_hbm.at[:, span], down_ref.at[slot], sems.at[0, slot]),
            pltpu.make_async_copy(gate_hbm.at[span, :], gate_ref.at[slot], sems.at[1, slot]),
            pltpu.make_async_copy(up_hbm.at[span, :], up_ref.at[slot], sems.at[2, slot]),
        )

    def body(j, slot):
        span = pl.ds(pl.multiple_of(j * step, step), step)
        result = nn_dot(hid_ref[...], down_ref[slot]).astype(BF)
        own_ref[0, :, span] = result[:half]
        other_ref[0, :, span] = result[half:]
        result = nt_dot(gb_ref[...], gate_ref[slot]) + nt_dot(ub_ref[...], up_ref[slot])
        result = result.astype(BF)
        own_ref[1, :, span] = result[:half]
        other_ref[1, :, span] = result[half:]

    streamed(gate_hbm.shape[0] // step, gate_ref.shape[0], copies, body)


def leave(hid, gb, ub, gate, up, down):
    rows, units = gb.shape
    width = gate.shape[0]
    half = rows // 2
    step = tile_of(width, (512, 256, 128))
    depth = min(DEPTH, width // step)
    return pl.pallas_call(
        lambda *refs: leave_kernel(step, *refs),
        in_specs=[VMEM] * 3 + [HBM] * 3,
        out_specs=[VMEM] * 2,
        out_shape=[shape((2, half, width))] * 2,
        scratch_shapes=[
            pltpu.VMEM((depth, step, units), BF),
            pltpu.VMEM((depth, step, units), BF),
            pltpu.VMEM((depth, units, step), BF),
            pltpu.SemaphoreType.DMA((3, depth)),
        ],
        compiler_params=grant((3 * depth * step, units, BF)),
        cost_estimate=cost(6 * rows * width * units, 6 * width * units),
        name="leave",
    )(hid, gb, ub, gate, up, down)


def rows_dot(left, right):
    return lax.dot_general(
        left, right, (((0,), (0,)), ((), ())), preferred_element_type=F32
    ).astype(BF)


def on_device(tokens, modality, gate, up, down, out_grad):
    count, width = out_grad.shape
    groups = lax.axis_size("seq")
    ring = lax.axis_size("dp") // CORES
    me = lax.axis_index("seq")
    part = width // groups

    def shift(value, k):
        return lax.ppermute(value, "dp", [
            (z * CORES + c, (z + k) % ring * CORES + c) for z in range(ring) for c in range(CORES)])

    def swap(value):
        return lax.ppermute(value, "dp", [
            (z * CORES + c, z * CORES + 1 - c) for z in range(ring) for c in range(CORES)])

    def across(value, mask):
        return lax.ppermute(value, "seq", [(g, g ^ mask) for g in range(groups)])

    def gathered(block):
        return jnp.concatenate([block] + [shift(block, k) for k in range(1, ring)], axis=0)

    def cut(matrix, group):
        return lax.dynamic_slice_in_dim(matrix, group * part, part, axis=1)

    def slices_of(tok_block, cot_block):
        def both(group):
            return jnp.concatenate([cut(tok_block, group), cut(cot_block, group)], axis=1)

        small = jnp.stack(
            [both(me)] + [across(both(me ^ m), m) for m in range(1, groups)])
        pieces = [small] + [shift(small, k) for k in range(1, ring)]
        own = jnp.stack(pieces, axis=1)
        mate = swap(own)
        both_cores = jnp.stack([own, mate], axis=1)
        return (both_cores[..., :part].reshape(-1, part), both_cores[..., part:].reshape(-1, part))

    def near(value):
        held = [[value]] + [None] * (groups - 1)
        for m in range(1, groups):
            if m & (m - 1) == 0:
                held[m] = [across(value, m)]
        return held

    def relay(held):
        half = held[0][0].shape[0] // 2
        held = list(held)
        for m in range(1, groups):
            low, high = m & -m, 1 << (m.bit_length() - 1)
            if low != high:
                a = jnp.concatenate(held[m ^ low], axis=0)
                b = jnp.concatenate(held[m ^ high], axis=0)
                held[m] = [across(a[:half], low), across(b[half:], high)]
        return held

    def after(values, others):
        leaves, tree = jax.tree.flatten(values)
        return jax.tree.unflatten(
            tree, lax.optimization_barrier((*leaves, *others))[:len(leaves)])

    def stack(held):
        return jnp.concatenate(sum(held, []), axis=0)

    block = pick(modality, tokens, count)
    tok = gathered(block)
    tok_mate = swap(tok)
    tok_all, cot_all = slices_of(block, out_grad)
    cot = gathered(out_grad)
    cot_mate = swap(cot)
    hid, active, factor = enter(tok, tok_mate, gate, up)
    all_hid = relay(near(hid))
    gb, ub = turn(cot, cot_mate, down, active, factor)
    all_gb = near(gb)
    all_ub = near(ub)
    own, other = leave(hid, gb, ub, gate, up, down)

    mate = swap(other)
    sums = (own.astype(F32) + mate.astype(F32)).astype(BF).reshape(2, ring, count, width)
    sums = [sums[:, k] for k in range(ring)]
    terms = [shift(sums[k], -k) for k in range(1, ring)]

    all_hid = after(all_hid, sums[1:])
    all_gb = relay(after(all_gb, sums[1:]))
    all_ub = relay(after(all_ub, sums[1:]))
    down_grad = rows_dot(stack(all_hid), cot_all)
    gate_grad = rows_dot(tok_all, stack(all_gb))
    up_grad = rows_dot(tok_all, stack(all_ub))
    terms = after(terms, [up_grad])
    total = sums[0].astype(F32)
    for term in terms:
        total = total + term.astype(F32)
    total = total.astype(BF)
    return total[0], total[1], gate_grad, up_grad, down_grad


def solution(mesh):
    rows = P(("dp", "seq"), None)
    return jax.shard_map(
        on_device,
        mesh=mesh,
        in_specs=(rows, P(("dp", "seq")), P(None, "dp"), P(None, "dp"), P("dp", None), rows),
        out_specs=(rows, rows, P("seq", "dp"), P("seq", "dp"), P("dp", "seq")),
        check_vma=False,
    )
```

```python
import jax
import jax.numpy as jnp
from jax import lax
from jax.experimental import pallas as pl
from jax.experimental.pallas import tpu as pltpu
from jax.sharding import PartitionSpec as P


BF = jnp.bfloat16
F32 = jnp.float32
CORES = 2
MIB = 1 << 20
ALL_VMEM = 67043328


HBM = pl.BlockSpec(memory_space=pltpu.HBM)
VMEM = pl.BlockSpec(memory_space=pltpu.VMEM)


def tile_of(extent, options):
    for option in options:
        if extent % option == 0:
            return option
    return extent


def cost(flops, nbytes):
    return pl.CostEstimate(flops=flops, bytes_accessed=nbytes, transcendentals=0)


def shape(dims, dtype=BF):
    return jax.ShapeDtypeStruct(dims, dtype)


def grant(*arrays, least=0):
    total = sum(2 * r * c if d == BF else 4 * r * c for r, c, d in arrays)
    return pltpu.CompilerParams(vmem_limit_bytes=min(max(total + 6 * MIB, least), ALL_VMEM))


def nt_dot(left, right):
    return lax.dot_general(left, right, (((1,), (1,)), ((), ())), preferred_element_type=F32)


def nn_dot(left, right):
    return jnp.dot(left, right, preferred_element_type=F32)


def pick_kernel(flag_hbm, tokens_hbm, out_ref, flag_ref, tokens_ref, sems):
    rows = out_ref.shape[0]
    count = tokens_ref.shape[0]
    copies = (pltpu.make_async_copy(flag_hbm, flag_ref, sems.at[0]),
              pltpu.make_async_copy(tokens_hbm, tokens_ref, sems.at[1]))
    for copy in copies:
        copy.start()
    for copy in copies:
        copy.wait()
    flags = (flag_ref[...] == 1).astype(F32)
    before = lax.broadcasted_iota(jnp.int32, (count, count), 0)
    after = lax.broadcasted_iota(jnp.int32, (count, count), 1)
    ranks = nn_dot(flags, (before <= after).astype(F32))
    slots = lax.broadcasted_iota(jnp.int32, (rows, count), 0).astype(F32) + 1.0
    chosen = (jnp.broadcast_to(ranks, (rows, count)) == slots) & (
        jnp.broadcast_to(flags, (rows, count)) == 1.0
    )
    out_ref[...] = nn_dot(chosen.astype(BF), tokens_ref[...]).astype(BF)


def pick(modality, tokens, rows):
    return pl.pallas_call(
        pick_kernel,
        in_specs=[HBM, HBM],
        out_specs=VMEM,
        out_shape=shape((rows, tokens.shape[1])),
        scratch_shapes=[
            pltpu.VMEM((1, modality.shape[0]), modality.dtype),
            pltpu.VMEM(tokens.shape, BF),
            pltpu.SemaphoreType.DMA((2,)),
        ],
        compiler_params=grant(least=ALL_VMEM),
        name="pick",
    )(modality.reshape(1, -1), tokens)


def streamed(steps, depth, copies, body):
    depth = min(depth, steps)

    def start(j):
        for copy in copies(j, lax.rem(j, depth)):
            copy.start()

    for j in range(depth):
        start(jnp.int32(j))

    @pl.loop(0, steps)
    def _(j):
        slot = lax.rem(j, depth)
        for copy in copies(j, slot):
            copy.wait()
        body(j, slot)

        @pl.when(j + depth < steps)
        def _():
            start(j + depth)


DEPTH = 5


def enter_kernel(tile, xa_ref, xb_ref, gate_hbm, up_hbm, hid_ref, active_ref, turn_ref,
                 x_ref, gate_ref, up_ref, sems):
    half = xa_ref.shape[0]
    x_ref[:half] = xa_ref[...]
    x_ref[half:] = xb_ref[...]

    def copies(j, slot):
        column = pl.ds(pl.multiple_of(j * tile, tile), tile)
        return (
            pltpu.make_async_copy(gate_hbm.at[:, column], gate_ref.at[slot], sems.at[0, slot]),
            pltpu.make_async_copy(up_hbm.at[:, column], up_ref.at[slot], sems.at[1, slot]),
        )

    def body(j, slot):
        column = pl.ds(pl.multiple_of(j * tile, tile), tile)
        gate_proj = nn_dot(x_ref[...], gate_ref[slot])
        up_proj = nn_dot(x_ref[...], up_ref[slot])
        sig = jax.nn.sigmoid(gate_proj)
        active = gate_proj * sig
        hid_ref[:, column] = (active * up_proj).astype(BF)
        active_ref[:, column] = active
        turn_ref[:, column] = up_proj * (sig * (1.0 + gate_proj * (1.0 - sig)))

    streamed(gate_hbm.shape[1] // tile, gate_ref.shape[0], copies, body)


def enter(own, other, gate, up):
    half, width = own.shape
    units = gate.shape[1]
    rows = 2 * half
    tile = tile_of(units, (256, 128))
    depth = min(DEPTH, units // tile)
    return pl.pallas_call(
        lambda *refs: enter_kernel(tile, *refs),
        in_specs=[VMEM, VMEM, HBM, HBM],
        out_specs=[VMEM] * 3,
        out_shape=[shape((rows, units)), shape((rows, units), F32), shape((rows, units), F32)],
        scratch_shapes=[
            pltpu.VMEM((rows, width), BF),
            pltpu.VMEM((depth, width, tile), BF),
            pltpu.VMEM((depth, width, tile), BF),
            pltpu.SemaphoreType.DMA((2, depth)),
        ],
        compiler_params=grant((rows, width, BF), (2 * depth * tile, width, BF), least=46 * MIB),
        cost_estimate=cost(4 * rows * width * units, 4 * width * units),
        name="enter",
    )(own, other, gate, up)


def turn_kernel(tile, ca_ref, cb_ref, down_hbm, active_ref, factor_ref, gb_ref, ub_ref,
                c_ref, down_ref, sems):
    half = ca_ref.shape[0]
    c_ref[:half] = ca_ref[...]
    c_ref[half:] = cb_ref[...]

    def copies(j, slot):
        row = pl.ds(pl.multiple_of(j * tile, tile), tile)
        return (pltpu.make_async_copy(down_hbm.at[row, :], down_ref.at[slot], sems.at[slot]),)

    def body(j, slot):
        span = pl.ds(pl.multiple_of(j * tile, tile), tile)
        back = nt_dot(c_ref[...], down_ref[slot])
        gb_ref[:, span] = (back * factor_ref[:, span]).astype(BF)
        ub_ref[:, span] = (back * active_ref[:, span]).astype(BF)

    streamed(down_hbm.shape[0] // tile, down_ref.shape[0], copies, body)


def turn(own, other, down, active, factor):
    half, width = own.shape
    units = down.shape[0]
    rows = 2 * half
    tile = tile_of(units, (256, 128))
    depth = min(DEPTH, units // tile)
    return pl.pallas_call(
        lambda *refs: turn_kernel(tile, *refs),
        in_specs=[VMEM, VMEM, HBM, VMEM, VMEM],
        out_specs=[VMEM] * 2,
        out_shape=[shape((rows, units))] * 2,
        scratch_shapes=[
            pltpu.VMEM((rows, width), BF),
            pltpu.VMEM((depth, tile, width), BF),
            pltpu.SemaphoreType.DMA((depth,)),
        ],
        compiler_params=grant((rows, width, BF), (depth * tile, width, BF), least=46 * MIB),
        cost_estimate=cost(2 * rows * width * units, 2 * width * units),
        name="turn",
    )(own, other, down, active, factor)


def leave_kernel(step, hid_ref, gb_ref, ub_ref, gate_hbm, up_hbm, down_hbm, own_ref, other_ref,
                 gate_ref, up_ref, down_ref, sems):
    half = own_ref.shape[1]

    def copies(j, slot):
        span = pl.ds(pl.multiple_of(j * step, step), step)
        return (
            pltpu.make_async_copy(down_hbm.at[:, span], down_ref.at[slot], sems.at[0, slot]),
            pltpu.make_async_copy(gate_hbm.at[span, :], gate_ref.at[slot], sems.at[1, slot]),
            pltpu.make_async_copy(up_hbm.at[span, :], up_ref.at[slot], sems.at[2, slot]),
        )

    def body(j, slot):
        span = pl.ds(pl.multiple_of(j * step, step), step)
        result = nn_dot(hid_ref[...], down_ref[slot]).astype(BF)
        own_ref[0, :, span] = result[:half]
        other_ref[0, :, span] = result[half:]
        result = nt_dot(gb_ref[...], gate_ref[slot]) + nt_dot(ub_ref[...], up_ref[slot])
        result = result.astype(BF)
        own_ref[1, :, span] = result[:half]
        other_ref[1, :, span] = result[half:]

    streamed(gate_hbm.shape[0] // step, gate_ref.shape[0], copies, body)


def leave(hid, gb, ub, gate, up, down):
    rows, units = gb.shape
    width = gate.shape[0]
    half = rows // 2
    step = tile_of(width, (512, 256, 128))
    depth = min(DEPTH, width // step)
    return pl.pallas_call(
        lambda *refs: leave_kernel(step, *refs),
        in_specs=[VMEM] * 3 + [HBM] * 3,
        out_specs=[VMEM] * 2,
        out_shape=[shape((2, half, width))] * 2,
        scratch_shapes=[
            pltpu.VMEM((depth, step, units), BF),
            pltpu.VMEM((depth, step, units), BF),
            pltpu.VMEM((depth, units, step), BF),
            pltpu.SemaphoreType.DMA((3, depth)),
        ],
        compiler_params=grant((3 * depth * step, units, BF), least=46 * MIB),
        cost_estimate=cost(6 * rows * width * units, 6 * width * units),
        name="leave",
    )(hid, gb, ub, gate, up, down)


def rows_dot(left, right):
    return lax.dot_general(
        left, right, (((0,), (0,)), ((), ())), preferred_element_type=F32
    ).astype(BF)


def on_device(tokens, modality, gate, up, down, out_grad):
    count, width = out_grad.shape
    groups = lax.axis_size("seq")
    ring = lax.axis_size("dp") // CORES
    me = lax.axis_index("seq")
    part = width // groups

    def shift(value, k):
        return lax.ppermute(value, "dp", [
            (z * CORES + c, (z + k) % ring * CORES + c) for z in range(ring) for c in range(CORES)])

    def swap(value):
        return lax.ppermute(value, "dp", [
            (z * CORES + c, z * CORES + 1 - c) for z in range(ring) for c in range(CORES)])

    def across(value, mask):
        return lax.ppermute(value, "seq", [(g, g ^ mask) for g in range(groups)])

    def gathered(block):
        return jnp.concatenate([block] + [shift(block, k) for k in range(1, ring)], axis=0)

    def cut(matrix, group):
        return lax.dynamic_slice_in_dim(matrix, group * part, part, axis=1)

    def slices_of(tok_block, cot_block):
        def both(group):
            return jnp.concatenate([cut(tok_block, group), cut(cot_block, group)], axis=1)

        small = jnp.stack(
            [both(me)] + [across(both(me ^ m), m) for m in range(1, groups)])
        pieces = [small] + [shift(small, k) for k in range(1, ring)]
        own = jnp.stack(pieces, axis=1)
        mate = swap(own)
        both_cores = jnp.stack([own, mate], axis=1)
        return (both_cores[..., :part].reshape(-1, part), both_cores[..., part:].reshape(-1, part))

    def near(value):
        held = [[value]] + [None] * (groups - 1)
        for m in range(1, groups):
            if m & (m - 1) == 0:
                held[m] = [across(value, m)]
        return held

    def relay(held):
        half = held[0][0].shape[0] // 2
        held = list(held)
        for m in range(1, groups):
            low, high = m & -m, 1 << (m.bit_length() - 1)
            if low != high:
                a = jnp.concatenate(held[m ^ low], axis=0)
                b = jnp.concatenate(held[m ^ high], axis=0)
                held[m] = [across(a[:half], low), across(b[half:], high)]
        return held

    def after(values, others):
        leaves, tree = jax.tree.flatten(values)
        return jax.tree.unflatten(
            tree, lax.optimization_barrier((*leaves, *others))[:len(leaves)])

    def stack(held):
        return jnp.concatenate(sum(held, []), axis=0)

    block = pick(modality, tokens, count)
    tok = gathered(block)
    tok_mate = swap(tok)
    tok_all, cot_all = slices_of(block, out_grad)
    cot = gathered(out_grad)
    cot_mate = swap(cot)
    hid, active, factor = enter(tok, tok_mate, gate, up)
    all_hid = relay(near(hid))
    gb, ub = turn(cot, cot_mate, down, active, factor)
    all_gb = near(gb)
    all_ub = near(ub)
    own, other = leave(hid, gb, ub, gate, up, down)

    mate = swap(other)
    sums = (own.astype(F32) + mate.astype(F32)).astype(BF).reshape(2, ring, count, width)
    sums = [sums[:, k] for k in range(ring)]
    terms = [shift(sums[k], -k) for k in range(1, ring)]

    all_hid = after(all_hid, sums[1:])
    all_gb = relay(after(all_gb, sums[1:]))
    all_ub = relay(after(all_ub, sums[1:]))
    down_grad = rows_dot(stack(all_hid), cot_all)
    gate_grad = rows_dot(tok_all, stack(all_gb))
    up_grad = rows_dot(tok_all, stack(all_ub))
    terms = after(terms, [up_grad])

    def total(side):
        value = sums[0][side].astype(F32)
        for term in terms:
            value = value + term[side].astype(F32)
        return value.astype(BF)

    output, in_grad = total(0), total(1)
    return output, in_grad, gate_grad, up_grad, down_grad


def solution(mesh):
    rows = P(("dp", "seq"), None)
    return jax.shard_map(
        on_device,
        mesh=mesh,
        in_specs=(rows, P(("dp", "seq")), P(None, "dp"), P(None, "dp"), P("dp", None), rows),
        out_specs=(rows, rows, P("seq", "dp"), P("seq", "dp"), P("dp", "seq")),
        check_vma=False,
    )
```

```python
import jax
import jax.numpy as jnp
from jax import lax
from jax.experimental import pallas as pl
from jax.experimental.pallas import tpu as pltpu
from jax.sharding import PartitionSpec as P


BF = jnp.bfloat16
F32 = jnp.float32
CORES = 2
MIB = 1 << 20
ALL_VMEM = 67043328


HBM = pl.BlockSpec(memory_space=pltpu.HBM)
VMEM = pl.BlockSpec(memory_space=pltpu.VMEM)


def tile_of(extent, options):
    for option in options:
        if extent % option == 0:
            return option
    return extent


def cost(flops, nbytes):
    return pl.CostEstimate(flops=flops, bytes_accessed=nbytes, transcendentals=0)


def shape(dims, dtype=BF):
    return jax.ShapeDtypeStruct(dims, dtype)


def grant(*arrays, least=0):
    total = sum(2 * r * c if d == BF else 4 * r * c for r, c, d in arrays)
    return pltpu.CompilerParams(vmem_limit_bytes=min(max(total + 6 * MIB, least), ALL_VMEM))


def nt_dot(left, right):
    return lax.dot_general(left, right, (((1,), (1,)), ((), ())), preferred_element_type=F32)


def nn_dot(left, right):
    return jnp.dot(left, right, preferred_element_type=F32)


def pick_kernel(flag_hbm, tokens_hbm, out_ref, left_ref, right_ref, flag_ref, tokens_ref, sems):
    rows = out_ref.shape[0]
    count = tokens_ref.shape[0]
    copies = (pltpu.make_async_copy(flag_hbm, flag_ref, sems.at[0]),
              pltpu.make_async_copy(tokens_hbm, tokens_ref, sems.at[1]))
    for copy in copies:
        copy.start()
    for copy in copies:
        copy.wait()
    flags = (flag_ref[...] == 1).astype(F32)
    before = lax.broadcasted_iota(jnp.int32, (count, count), 0)
    after = lax.broadcasted_iota(jnp.int32, (count, count), 1)
    ranks = nn_dot(flags, (before <= after).astype(F32))
    slots = lax.broadcasted_iota(jnp.int32, (rows, count), 0).astype(F32) + 1.0
    chosen = (jnp.broadcast_to(ranks, (rows, count)) == slots) & (
        jnp.broadcast_to(flags, (rows, count)) == 1.0
    )
    picked = nn_dot(chosen.astype(BF), tokens_ref[...]).astype(BF)
    middle = left_ref.shape[1]
    out_ref[...] = picked
    left_ref[...] = picked[:, :middle]
    right_ref[...] = picked[:, middle:]


def pick(modality, tokens, rows):
    width = tokens.shape[1]
    return pl.pallas_call(
        pick_kernel,
        in_specs=[HBM, HBM],
        out_specs=[VMEM] * 3,
        out_shape=[shape((rows, width)), shape((rows, width // 2)), shape((rows, width // 2))],
        scratch_shapes=[
            pltpu.VMEM((1, modality.shape[0]), modality.dtype),
            pltpu.VMEM(tokens.shape, BF),
            pltpu.SemaphoreType.DMA((2,)),
        ],
        compiler_params=grant(least=ALL_VMEM),
        name="pick",
    )(modality.reshape(1, -1), tokens)


def streamed(steps, depth, copies, body, first):
    depth = min(depth, steps)

    def start(j):
        for copy in copies(j, lax.rem(j, depth)):
            copy.start()

    for j in range(depth):
        start(jnp.int32(j))
    first()

    @pl.loop(0, steps)
    def _(j):
        slot = lax.rem(j, depth)
        for copy in copies(j, slot):
            copy.wait()
        body(j, slot)

        @pl.when(j + depth < steps)
        def _():
            start(j + depth)


DEPTH = 5


def enter_kernel(tile, last, xa_ref, xb_ref, gate_hbm, up_hbm, *refs):
    (*before, hid_ref, active_ref, turn_ref) = refs[:5] if last else (None, *refs[:2])
    x_ref, gate_ref, up_ref, sems = refs[5:] if last else refs[2:]
    half, depth = xa_ref.shape
    rows = pl.ds(depth if last else 0, depth)

    def first():
        x_ref[:half] = xa_ref[...]
        x_ref[half:] = xb_ref[...]

    def copies(j, slot):
        column = pl.ds(pl.multiple_of(j * tile, tile), tile)
        return (
            pltpu.make_async_copy(gate_hbm.at[rows, column], gate_ref.at[slot], sems.at[0, slot]),
            pltpu.make_async_copy(up_hbm.at[rows, column], up_ref.at[slot], sems.at[1, slot]),
        )

    def body(j, slot):
        column = pl.ds(pl.multiple_of(j * tile, tile), tile)
        gate_proj = nn_dot(x_ref[...], gate_ref[slot])
        up_proj = nn_dot(x_ref[...], up_ref[slot])
        if not last:
            active_ref[:, column] = gate_proj
            turn_ref[:, column] = up_proj
            return
        gate_proj = gate_proj + before[0][:, column]
        up_proj = up_proj + before[1][:, column]
        sig = jax.nn.sigmoid(gate_proj)
        active = gate_proj * sig
        hid_ref[:, column] = (active * up_proj).astype(BF)
        active_ref[:, column] = active
        turn_ref[:, column] = up_proj * (sig * (1.0 + gate_proj * (1.0 - sig)))

    streamed(gate_hbm.shape[1] // tile, gate_ref.shape[0], copies, body, first)


def enter(own, other, gate, up, *before):
    half, width = own.shape
    units = gate.shape[1]
    rows = 2 * half
    tile = tile_of(units, (256, 128))
    depth = min(DEPTH, units // tile)
    last = len(before) > 0
    wide = shape((rows, units), F32)
    outs = [shape((rows, units)), wide, wide] if last else [wide, wide]
    return pl.pallas_call(
        lambda *refs: enter_kernel(tile, last, *refs),
        in_specs=[VMEM, VMEM, HBM, HBM] + [VMEM] * len(before),
        out_specs=[VMEM] * len(outs),
        out_shape=outs,
        scratch_shapes=[
            pltpu.VMEM((rows, width), BF),
            pltpu.VMEM((depth, width, tile), BF),
            pltpu.VMEM((depth, width, tile), BF),
            pltpu.SemaphoreType.DMA((2, depth)),
        ],
        compiler_params=grant((rows, width, BF), (2 * depth * tile, width, BF), least=46 * MIB),
        cost_estimate=cost(4 * rows * width * units, 4 * width * units),
        name="enter",
    )(own, other, gate, up, *before)


def turn_kernel(tile, ca_ref, cb_ref, down_hbm, active_ref, factor_ref, gb_ref, ub_ref,
                c_ref, down_ref, sems):
    half = ca_ref.shape[0]

    def first():
        c_ref[:half] = ca_ref[...]
        c_ref[half:] = cb_ref[...]

    def copies(j, slot):
        row = pl.ds(pl.multiple_of(j * tile, tile), tile)
        return (pltpu.make_async_copy(down_hbm.at[row, :], down_ref.at[slot], sems.at[slot]),)

    def body(j, slot):
        span = pl.ds(pl.multiple_of(j * tile, tile), tile)
        back = nt_dot(c_ref[...], down_ref[slot])
        gb_ref[:, span] = (back * factor_ref[:, span]).astype(BF)
        ub_ref[:, span] = (back * active_ref[:, span]).astype(BF)

    streamed(down_hbm.shape[0] // tile, down_ref.shape[0], copies, body, first)


def turn(own, other, down, active, factor):
    half, width = own.shape
    units = down.shape[0]
    rows = 2 * half
    tile = tile_of(units, (256, 128))
    depth = min(DEPTH, units // tile)
    return pl.pallas_call(
        lambda *refs: turn_kernel(tile, *refs),
        in_specs=[VMEM, VMEM, HBM, VMEM, VMEM],
        out_specs=[VMEM] * 2,
        out_shape=[shape((rows, units))] * 2,
        scratch_shapes=[
            pltpu.VMEM((rows, width), BF),
            pltpu.VMEM((depth, tile, width), BF),
            pltpu.SemaphoreType.DMA((depth,)),
        ],
        compiler_params=grant((rows, width, BF), (depth * tile, width, BF), least=46 * MIB),
        cost_estimate=cost(2 * rows * width * units, 2 * width * units),
        name="turn",
    )(own, other, down, active, factor)


def leave_kernel(step, hid_ref, gb_ref, ub_ref, gate_hbm, up_hbm, down_hbm, own_ref, other_ref,
                 gate_ref, up_ref, down_ref, sems):
    half = own_ref.shape[1]

    def copies(j, slot):
        span = pl.ds(pl.multiple_of(j * step, step), step)
        return (
            pltpu.make_async_copy(down_hbm.at[:, span], down_ref.at[slot], sems.at[0, slot]),
            pltpu.make_async_copy(gate_hbm.at[span, :], gate_ref.at[slot], sems.at[1, slot]),
            pltpu.make_async_copy(up_hbm.at[span, :], up_ref.at[slot], sems.at[2, slot]),
        )

    def body(j, slot):
        span = pl.ds(pl.multiple_of(j * step, step), step)
        result = nn_dot(hid_ref[...], down_ref[slot]).astype(BF)
        own_ref[0, :, span] = result[:half]
        other_ref[0, :, span] = result[half:]
        result = nt_dot(gb_ref[...], gate_ref[slot]) + nt_dot(ub_ref[...], up_ref[slot])
        result = result.astype(BF)
        own_ref[1, :, span] = result[:half]
        other_ref[1, :, span] = result[half:]

    streamed(gate_hbm.shape[0] // step, gate_ref.shape[0], copies, body, lambda: None)


def leave(hid, gb, ub, gate, up, down):
    rows, units = gb.shape
    width = gate.shape[0]
    half = rows // 2
    step = tile_of(width, (512, 256, 128))
    depth = min(DEPTH, width // step)
    return pl.pallas_call(
        lambda *refs: leave_kernel(step, *refs),
        in_specs=[VMEM] * 3 + [HBM] * 3,
        out_specs=[VMEM] * 2,
        out_shape=[shape((2, half, width))] * 2,
        scratch_shapes=[
            pltpu.VMEM((depth, step, units), BF),
            pltpu.VMEM((depth, step, units), BF),
            pltpu.VMEM((depth, units, step), BF),
            pltpu.SemaphoreType.DMA((3, depth)),
        ],
        compiler_params=grant((3 * depth * step, units, BF), least=46 * MIB),
        cost_estimate=cost(6 * rows * width * units, 6 * width * units),
        name="leave",
    )(hid, gb, ub, gate, up, down)


def rows_dot(left, right):
    return lax.dot_general(
        left, right, (((0,), (0,)), ((), ())), preferred_element_type=F32
    ).astype(BF)


def on_device(tokens, modality, gate, up, down, out_grad):
    count, width = out_grad.shape
    groups = lax.axis_size("seq")
    ring = lax.axis_size("dp") // CORES
    me = lax.axis_index("seq")
    part = width // groups

    def shift(value, k):
        return lax.ppermute(value, "dp", [
            (z * CORES + c, (z + k) % ring * CORES + c) for z in range(ring) for c in range(CORES)])

    def swap(value):
        return lax.ppermute(value, "dp", [
            (z * CORES + c, z * CORES + 1 - c) for z in range(ring) for c in range(CORES)])

    def across(value, mask):
        return lax.ppermute(value, "seq", [(g, g ^ mask) for g in range(groups)])

    def gathered(block):
        return jnp.concatenate([block] + [shift(block, k) for k in range(1, ring)], axis=0)

    def cut(matrix, group):
        return lax.dynamic_slice_in_dim(matrix, group * part, part, axis=1)

    def slices_of(tok_block, cot_block):
        def both(group):
            return jnp.concatenate([cut(tok_block, group), cut(cot_block, group)], axis=1)

        small = jnp.stack(
            [both(me)] + [across(both(me ^ m), m) for m in range(1, groups)])
        pieces = [small] + [shift(small, k) for k in range(1, ring)]
        own = jnp.stack(pieces, axis=1)
        mate = swap(own)
        both_cores = jnp.stack([own, mate], axis=1)
        return (both_cores[..., :part].reshape(-1, part), both_cores[..., part:].reshape(-1, part))

    def near(value):
        held = [[value]] + [None] * (groups - 1)
        for m in range(1, groups):
            if m & (m - 1) == 0:
                held[m] = [across(value, m)]
        return held

    def relay(held):
        half = held[0][0].shape[0] // 2
        held = list(held)
        for m in range(1, groups):
            low, high = m & -m, 1 << (m.bit_length() - 1)
            if low != high:
                a = jnp.concatenate(held[m ^ low], axis=0)
                b = jnp.concatenate(held[m ^ high], axis=0)
                held[m] = [across(a[:half], low), across(b[half:], high)]
        return held

    def after(values, others):
        leaves, tree = jax.tree.flatten(values)
        return jax.tree.unflatten(
            tree, lax.optimization_barrier((*leaves, *others))[:len(leaves)])

    def stack(held):
        return jnp.concatenate(sum(held, []), axis=0)

    block, *sides = pick(modality, tokens, count)
    tok = [gathered(side) for side in sides]
    tok_mate = []
    for side in tok:
        tok_mate.append(swap(side))
    tok_all, cot_all = slices_of(block, out_grad)
    cot = gathered(out_grad)
    cot_mate = swap(cot)
    before = enter(tok[0], tok_mate[0], gate, up)
    hid, active, factor = enter(tok[1], tok_mate[1], gate, up, *before)
    all_hid = relay(near(hid))
    gb, ub = turn(cot, cot_mate, down, active, factor)
    all_gb = near(gb)
    all_ub = near(ub)
    own, other = leave(hid, gb, ub, gate, up, down)

    mate = swap(other)
    sums = (own.astype(F32) + mate.astype(F32)).astype(BF).reshape(2, ring, count, width)
    sums = [sums[:, k] for k in range(ring)]
    terms = [shift(sums[k], -k) for k in range(1, ring)]

    all_hid = after(all_hid, sums[1:])
    all_gb = relay(after(all_gb, sums[1:]))
    all_ub = relay(after(all_ub, sums[1:]))
    down_grad = rows_dot(stack(all_hid), cot_all)
    gate_grad = rows_dot(tok_all, stack(all_gb))
    up_grad = rows_dot(tok_all, stack(all_ub))
    terms = after(terms, [up_grad])

    def total(side):
        value = sums[0][side].astype(F32)
        for term in terms:
            value = value + term[side].astype(F32)
        return value.astype(BF)

    output, in_grad = total(0), total(1)
    return output, in_grad, gate_grad, up_grad, down_grad


def solution(mesh):
    rows = P(("dp", "seq"), None)
    return jax.shard_map(
        on_device,
        mesh=mesh,
        in_specs=(rows, P(("dp", "seq")), P(None, "dp"), P(None, "dp"), P("dp", None), rows),
        out_specs=(rows, rows, P("seq", "dp"), P("seq", "dp"), P("dp", "seq")),
        check_vma=False,
    )
```

```python
import jax
import jax.numpy as jnp
from jax import lax
from jax.experimental import pallas as pl
from jax.experimental.pallas import tpu as pltpu
from jax.sharding import PartitionSpec as P


BF = jnp.bfloat16
F32 = jnp.float32
CORES = 2
MIB = 1 << 20
ALL_VMEM = 67043328


HBM = pl.BlockSpec(memory_space=pltpu.HBM)
VMEM = pl.BlockSpec(memory_space=pltpu.VMEM)


def tile_of(extent, options):
    for option in options:
        if extent % option == 0:
            return option
    return extent


def cost(flops, nbytes):
    return pl.CostEstimate(flops=flops, bytes_accessed=nbytes, transcendentals=0)


def shape(dims, dtype=BF):
    return jax.ShapeDtypeStruct(dims, dtype)


def grant(*arrays, least=0):
    total = sum(2 * r * c if d == BF else 4 * r * c for r, c, d in arrays)
    return pltpu.CompilerParams(vmem_limit_bytes=min(max(total + 6 * MIB, least), ALL_VMEM))


def nt_dot(left, right):
    return lax.dot_general(left, right, (((1,), (1,)), ((), ())), preferred_element_type=F32)


def nn_dot(left, right):
    return jnp.dot(left, right, preferred_element_type=F32)


def pick_kernel(flag_hbm, tokens_hbm, out_ref, left_ref, right_ref, flag_ref, tokens_ref, sems):
    rows = out_ref.shape[0]
    count = tokens_ref.shape[0]
    copies = (pltpu.make_async_copy(flag_hbm, flag_ref, sems.at[0]),
              pltpu.make_async_copy(tokens_hbm, tokens_ref, sems.at[1]))
    for copy in copies:
        copy.start()
    for copy in copies:
        copy.wait()
    flags = (flag_ref[...] == 1).astype(F32)
    before = lax.broadcasted_iota(jnp.int32, (count, count), 0)
    after = lax.broadcasted_iota(jnp.int32, (count, count), 1)
    ranks = nn_dot(flags, (before <= after).astype(F32))
    slots = lax.broadcasted_iota(jnp.int32, (rows, count), 0).astype(F32) + 1.0
    chosen = (jnp.broadcast_to(ranks, (rows, count)) == slots) & (
        jnp.broadcast_to(flags, (rows, count)) == 1.0
    )
    picked = nn_dot(chosen.astype(BF), tokens_ref[...]).astype(BF)
    middle = left_ref.shape[1]
    out_ref[...] = picked
    left_ref[...] = picked[:, :middle]
    right_ref[...] = picked[:, middle:]


def pick(modality, tokens, rows):
    width = tokens.shape[1]
    return pl.pallas_call(
        pick_kernel,
        in_specs=[HBM, HBM],
        out_specs=[VMEM] * 3,
        out_shape=[shape((rows, width)), shape((rows, width // 2)), shape((rows, width // 2))],
        scratch_shapes=[
            pltpu.VMEM((1, modality.shape[0]), modality.dtype),
            pltpu.VMEM(tokens.shape, BF),
            pltpu.SemaphoreType.DMA((2,)),
        ],
        compiler_params=grant(least=ALL_VMEM),
        name="pick",
    )(modality.reshape(1, -1), tokens)


def streamed(steps, depth, copies, body, first):
    depth = min(depth, steps)

    def start(j):
        for copy in copies(j, lax.rem(j, depth)):
            copy.start()

    for j in range(depth):
        start(jnp.int32(j))
    first()

    @pl.loop(0, steps)
    def _(j):
        slot = lax.rem(j, depth)
        for copy in copies(j, slot):
            copy.wait()
        body(j, slot)

        @pl.when(j + depth < steps)
        def _():
            start(j + depth)


DEPTH = 5


def enter_kernel(tile, last, xa_ref, xb_ref, gate_hbm, up_hbm, *refs):
    (*before, hid_ref, active_ref, turn_ref) = refs[:5] if last else (None, *refs[:2])
    x_ref, gate_ref, up_ref, sems = refs[5:] if last else refs[2:]
    half, depth = xa_ref.shape
    rows = pl.ds(depth if last else 0, depth)

    def first():
        x_ref[:half] = xa_ref[...]
        x_ref[half:] = xb_ref[...]

    def copies(j, slot):
        column = pl.ds(pl.multiple_of(j * tile, tile), tile)
        return (
            pltpu.make_async_copy(gate_hbm.at[rows, column], gate_ref.at[slot], sems.at[0, slot]),
            pltpu.make_async_copy(up_hbm.at[rows, column], up_ref.at[slot], sems.at[1, slot]),
        )

    def body(j, slot):
        column = pl.ds(pl.multiple_of(j * tile, tile), tile)
        gate_proj = nn_dot(x_ref[...], gate_ref[slot])
        up_proj = nn_dot(x_ref[...], up_ref[slot])
        if not last:
            active_ref[:, column] = gate_proj
            turn_ref[:, column] = up_proj
            return
        gate_proj = gate_proj + before[0][:, column]
        up_proj = up_proj + before[1][:, column]
        sig = jax.nn.sigmoid(gate_proj)
        active = gate_proj * sig
        hid_ref[:, column] = (active * up_proj).astype(BF)
        active_ref[:, column] = active
        turn_ref[:, column] = up_proj * (sig * (1.0 + gate_proj * (1.0 - sig)))

    streamed(gate_hbm.shape[1] // tile, gate_ref.shape[0], copies, body, first)


def enter(own, other, gate, up, *before):
    half, width = own.shape
    units = gate.shape[1]
    rows = 2 * half
    tile = tile_of(units, (256, 128))
    depth = min(DEPTH, units // tile)
    last = len(before) > 0
    wide = shape((rows, units), F32)
    outs = [shape((rows, units)), wide, wide] if last else [wide, wide]
    return pl.pallas_call(
        lambda *refs: enter_kernel(tile, last, *refs),
        in_specs=[VMEM, VMEM, HBM, HBM] + [VMEM] * len(before),
        out_specs=[VMEM] * len(outs),
        out_shape=outs,
        scratch_shapes=[
            pltpu.VMEM((rows, width), BF),
            pltpu.VMEM((depth, width, tile), BF),
            pltpu.VMEM((depth, width, tile), BF),
            pltpu.SemaphoreType.DMA((2, depth)),
        ],
        compiler_params=grant((rows, width, BF), (2 * depth * tile, width, BF), least=46 * MIB),
        cost_estimate=cost(4 * rows * width * units, 4 * width * units),
        name="enter",
    )(own, other, gate, up, *before)


def turn_kernel(tile, ca_ref, cb_ref, down_hbm, active_ref, factor_ref, gb_ref, ub_ref,
                c_ref, down_ref, sems):
    half = ca_ref.shape[0]

    def first():
        c_ref[:half] = ca_ref[...]
        c_ref[half:] = cb_ref[...]

    def copies(j, slot):
        row = pl.ds(pl.multiple_of(j * tile, tile), tile)
        return (pltpu.make_async_copy(down_hbm.at[row, :], down_ref.at[slot], sems.at[slot]),)

    def body(j, slot):
        span = pl.ds(pl.multiple_of(j * tile, tile), tile)
        back = nt_dot(c_ref[...], down_ref[slot])
        gb_ref[:, span] = (back * factor_ref[:, span]).astype(BF)
        ub_ref[:, span] = (back * active_ref[:, span]).astype(BF)

    streamed(down_hbm.shape[0] // tile, down_ref.shape[0], copies, body, first)


def turn(own, other, down, active, factor):
    half, width = own.shape
    units = down.shape[0]
    rows = 2 * half
    tile = tile_of(units, (256, 128))
    depth = min(DEPTH, units // tile)
    return pl.pallas_call(
        lambda *refs: turn_kernel(tile, *refs),
        in_specs=[VMEM, VMEM, HBM, VMEM, VMEM],
        out_specs=[VMEM] * 2,
        out_shape=[shape((rows, units))] * 2,
        scratch_shapes=[
            pltpu.VMEM((rows, width), BF),
            pltpu.VMEM((depth, tile, width), BF),
            pltpu.SemaphoreType.DMA((depth,)),
        ],
        compiler_params=grant((rows, width, BF), (depth * tile, width, BF), least=46 * MIB),
        cost_estimate=cost(2 * rows * width * units, 2 * width * units),
        name="turn",
    )(own, other, down, active, factor)


def leave_kernel(step, hid_ref, gb_ref, ub_ref, gate_hbm, up_hbm, down_hbm, own_ref, other_ref,
                 gate_ref, up_ref, down_ref, sems):
    half = own_ref.shape[1]

    def copies(j, slot):
        span = pl.ds(pl.multiple_of(j * step, step), step)
        return (
            pltpu.make_async_copy(down_hbm.at[:, span], down_ref.at[slot], sems.at[0, slot]),
            pltpu.make_async_copy(gate_hbm.at[span, :], gate_ref.at[slot], sems.at[1, slot]),
            pltpu.make_async_copy(up_hbm.at[span, :], up_ref.at[slot], sems.at[2, slot]),
        )

    def body(j, slot):
        span = pl.ds(pl.multiple_of(j * step, step), step)
        result = nn_dot(hid_ref[...], down_ref[slot]).astype(BF)
        own_ref[0, :, span] = result[:half]
        other_ref[0, :, span] = result[half:]
        result = nt_dot(gb_ref[...], gate_ref[slot]) + nt_dot(ub_ref[...], up_ref[slot])
        result = result.astype(BF)
        own_ref[1, :, span] = result[:half]
        other_ref[1, :, span] = result[half:]

    streamed(gate_hbm.shape[0] // step, gate_ref.shape[0], copies, body, lambda: None)


def leave(hid, gb, ub, gate, up, down):
    rows, units = gb.shape
    width = gate.shape[0]
    half = rows // 2
    step = tile_of(width, (512, 256, 128))
    depth = min(DEPTH, width // step)
    return pl.pallas_call(
        lambda *refs: leave_kernel(step, *refs),
        in_specs=[VMEM] * 3 + [HBM] * 3,
        out_specs=[VMEM] * 2,
        out_shape=[shape((2, half, width))] * 2,
        scratch_shapes=[
            pltpu.VMEM((depth, step, units), BF),
            pltpu.VMEM((depth, step, units), BF),
            pltpu.VMEM((depth, units, step), BF),
            pltpu.SemaphoreType.DMA((3, depth)),
        ],
        compiler_params=grant((3 * depth * step, units, BF), least=40 * MIB),
        cost_estimate=cost(6 * rows * width * units, 6 * width * units),
        name="leave",
    )(hid, gb, ub, gate, up, down)


def fold_kernel(first_ref, own_ref, mate_ref, *chunks):
    count = chunks[0].shape[1]
    ring = own_ref.shape[1] // count
    for k in range(ring):
        span = slice(k * count, (k + 1) * count)
        both = own_ref[:, span].astype(F32) + mate_ref[:, span].astype(F32)
        chunks[k][...] = both.astype(BF)
    if len(chunks) > ring:
        @pl.when(first_ref[0] == 1)
        def _():
            chunks[ring][...] = chunks[1][...]

        @pl.when(first_ref[0] != 1)
        def _():
            chunks[ring][...] = chunks[ring - 1][...]


def fold(first, own, mate, ring, chunks):
    sides, rows, width = own.shape
    return pl.pallas_call(
        fold_kernel,
        in_specs=[pl.BlockSpec(memory_space=pltpu.SMEM), VMEM, VMEM],
        out_specs=[VMEM] * chunks,
        out_shape=[shape((sides, rows // ring, width))] * chunks,
        compiler_params=grant(),
        cost_estimate=cost(own.size, 6 * own.size),
        name="fold",
    )(first, own, mate)


def rows_dot(left, right):
    return lax.dot_general(
        left, right, (((0,), (0,)), ((), ())), preferred_element_type=F32
    ).astype(BF)


def on_device(tokens, modality, gate, up, down, out_grad):
    count, width = out_grad.shape
    groups = lax.axis_size("seq")
    ring = lax.axis_size("dp") // CORES
    part = width // groups
    starts = [(lax.axis_index("seq") ^ m) * part for m in range(groups)]
    first = (lax.axis_index("dp") < CORES).astype(jnp.int32).reshape(1)
    tokens, modality, first, *starts = lax.optimization_barrier(
        (tokens, modality, first, *starts))

    def shift(value, k):
        return lax.ppermute(value, "dp", [
            (z * CORES + c, (z + k) % ring * CORES + c) for z in range(ring) for c in range(CORES)])

    def swap(value):
        return lax.ppermute(value, "dp", [
            (z * CORES + c, z * CORES + 1 - c) for z in range(ring) for c in range(CORES)])

    def across(value, mask):
        return lax.ppermute(value, "seq", [(g, g ^ mask) for g in range(groups)])

    def gathered(block):
        return jnp.concatenate([block] + [shift(block, k) for k in range(1, ring)], axis=0)

    def cut(matrix, m):
        return lax.dynamic_slice_in_dim(matrix, starts[m], part, axis=1)

    def slices_of(tok_block, cot_block):
        def both(m):
            return jnp.concatenate([cut(tok_block, m), cut(cot_block, m)], axis=1)

        small = jnp.stack([both(0)] + [across(both(m), m) for m in range(1, groups)])
        pieces = [small] + [shift(small, k) for k in range(1, ring)]
        own = jnp.stack(pieces, axis=1)
        mate = swap(own)
        both_cores = jnp.stack([own, mate], axis=1)
        return (both_cores[..., :part].reshape(-1, part), both_cores[..., part:].reshape(-1, part))

    def near(value):
        held = [[value]] + [None] * (groups - 1)
        for m in range(1, groups):
            if m & (m - 1) == 0:
                held[m] = [across(value, m)]
        return held

    def relay(held):
        half = held[0][0].shape[0] // 2
        held = list(held)
        for m in range(1, groups):
            low, high = m & -m, 1 << (m.bit_length() - 1)
            if low != high:
                a = jnp.concatenate(held[m ^ low], axis=0)
                b = jnp.concatenate(held[m ^ high], axis=0)
                held[m] = [across(a[:half], low), across(b[half:], high)]
        return held

    def after(values, others):
        leaves, tree = jax.tree.flatten(values)
        return jax.tree.unflatten(
            tree, lax.optimization_barrier((*leaves, *others))[:len(leaves)])

    def returned(own, mate):
        line = ring == 4
        sums = fold(first, own, mate, ring, ring + line)
        if not line:
            return [sums[0]] + [shift(sums[k], -k) for k in range(1, ring)]

        def along(value, pairs):
            return lax.ppermute(value, "dp", [
                (a * CORES + c, b * CORES + c) for a, b in pairs for c in range(CORES)])

        far = along(sums[4], [(0, 1), (3, 2)])
        terms = [along(sums[1], [(1, 0), (2, 1), (3, 2)]),
                 along(sums[3], [(0, 1), (1, 2), (2, 3)])]
        mid = (sums[2].astype(F32) + far.astype(F32)).astype(BF)
        return [sums[0], *terms, shift(mid, 2)]

    def stack(held):
        return jnp.concatenate(sum(held, []), axis=0)

    block, *sides = pick(modality, tokens, count)
    tok = [gathered(side) for side in sides]
    tok_mate = []
    for side in tok:
        tok_mate.append(swap(side))
    tok_all, cot_all = slices_of(block, out_grad)
    cot = gathered(out_grad)
    cot_mate = swap(cot)
    before = enter(tok[0], tok_mate[0], gate, up)
    hid, active, factor = enter(tok[1], tok_mate[1], gate, up, *before)
    all_hid = relay(near(hid))
    gb, ub = turn(cot, cot_mate, down, active, factor)
    all_gb = near(gb)
    all_ub = near(ub)
    own, other = leave(hid, gb, ub, gate, up, down)

    mate = swap(other)
    terms = returned(own, mate)
    all_hid = after(all_hid, terms[:1])
    all_gb = relay(all_gb)
    all_ub = relay(after(all_ub, terms[:1]))
    down_grad = rows_dot(stack(all_hid), cot_all)
    gate_grad = rows_dot(tok_all, stack(all_gb))
    up_grad = rows_dot(tok_all, stack(all_ub))
    terms = after(terms, [up_grad])

    def total(side):
        value = terms[0][side].astype(F32)
        for term in terms[1:]:
            value = value + term[side].astype(F32)
        return value.astype(BF)

    output, in_grad = total(0), total(1)
    return output, in_grad, gate_grad, up_grad, down_grad


def solution(mesh):
    rows = P(("dp", "seq"), None)
    return jax.shard_map(
        on_device,
        mesh=mesh,
        in_specs=(rows, P(("dp", "seq")), P(None, "dp"), P(None, "dp"), P("dp", None), rows),
        out_specs=(rows, rows, P("seq", "dp"), P("seq", "dp"), P("dp", "seq")),
        check_vma=False,
    )
```

```python
import jax
import jax.numpy as jnp
from jax import lax
from jax.experimental import pallas as pl
from jax.experimental.pallas import tpu as pltpu
from jax.sharding import PartitionSpec as P


BF = jnp.bfloat16
F32 = jnp.float32
CORES = 2
MIB = 1 << 20
ALL_VMEM = 67043328


HBM = pl.BlockSpec(memory_space=pltpu.HBM)
VMEM = pl.BlockSpec(memory_space=pltpu.VMEM)


def tile_of(extent, options):
    for option in options:
        if extent % option == 0:
            return option
    return extent


def cost(flops, nbytes):
    return pl.CostEstimate(flops=flops, bytes_accessed=nbytes, transcendentals=0)


def shape(dims, dtype=BF):
    return jax.ShapeDtypeStruct(dims, dtype)


def grant(*arrays, least=0):
    total = sum(2 * r * c if d == BF else 4 * r * c for r, c, d in arrays)
    return pltpu.CompilerParams(vmem_limit_bytes=min(max(total + 6 * MIB, least), ALL_VMEM))


def nt_dot(left, right):
    return lax.dot_general(left, right, (((1,), (1,)), ((), ())), preferred_element_type=F32)


def nn_dot(left, right):
    return jnp.dot(left, right, preferred_element_type=F32)


def pick_kernel(seat_ref, flag_ref, tokens_ref, cot_ref, left_ref, right_ref, *refs):
    blocks, picked_ref = refs[:-1], refs[-1]
    rows = cot_ref.shape[0]
    count = tokens_ref.shape[0]
    flags = (flag_ref[...] == 1).astype(F32)
    before = lax.broadcasted_iota(jnp.int32, (count, count), 0)
    after = lax.broadcasted_iota(jnp.int32, (count, count), 1)
    ranks = nn_dot(flags, (before <= after).astype(F32))
    slots = lax.broadcasted_iota(jnp.int32, (rows, count), 0).astype(F32) + 1.0
    chosen = (jnp.broadcast_to(ranks, (rows, count)) == slots) & (
        jnp.broadcast_to(flags, (rows, count)) == 1.0
    )
    picked_ref[...] = nn_dot(chosen.astype(BF), tokens_ref[...]).astype(BF)
    middle = left_ref.shape[1]
    left_ref[...] = picked_ref[:, :middle]
    right_ref[...] = picked_ref[:, middle:]
    part = picked_ref.shape[1] // len(blocks)
    for m, block in enumerate(blocks):
        span = pl.ds(pl.multiple_of((seat_ref[0] ^ m) * part, part), part)
        block[:, :part] = picked_ref[:, span]
        block[:, part:] = cot_ref[:, span]


def pick(seat, modality, tokens, out_grad, groups):
    rows, width = out_grad.shape
    half, block = shape((rows, width // 2)), shape((rows, 2 * width // groups))
    return pl.pallas_call(
        pick_kernel,
        in_specs=[pl.BlockSpec(memory_space=pltpu.SMEM)] + [VMEM] * 3,
        out_specs=[VMEM] * (2 + groups),
        out_shape=[half, half] + [block] * groups,
        scratch_shapes=[pltpu.VMEM((rows, width), BF)],
        compiler_params=grant(),
        name="pick",
    )(seat, modality.reshape(1, -1), tokens, out_grad)


def streamed(steps, depth, copies, body, first):
    depth = min(depth, steps)

    def start(j):
        for copy in copies(j, lax.rem(j, depth)):
            copy.start()

    for j in range(depth):
        start(jnp.int32(j))
    first()

    @pl.loop(0, steps)
    def _(j):
        slot = lax.rem(j, depth)
        for copy in copies(j, slot):
            copy.wait()
        body(j, slot)

        @pl.when(j + depth < steps)
        def _():
            start(j + depth)


DEPTH = 5


def enter_kernel(tile, last, xa_ref, xb_ref, gate_hbm, up_hbm, *refs):
    (*before, hid_ref, active_ref, turn_ref) = refs[:5] if last else (None, *refs[:2])
    x_ref, gate_ref, up_ref, sems = refs[5:] if last else refs[2:]
    half, depth = xa_ref.shape
    rows = pl.ds(depth if last else 0, depth)

    def first():
        x_ref[:half] = xa_ref[...]
        x_ref[half:] = xb_ref[...]

    def copies(j, slot):
        column = pl.ds(pl.multiple_of(j * tile, tile), tile)
        return (
            pltpu.make_async_copy(gate_hbm.at[rows, column], gate_ref.at[slot], sems.at[0, slot]),
            pltpu.make_async_copy(up_hbm.at[rows, column], up_ref.at[slot], sems.at[1, slot]),
        )

    def body(j, slot):
        column = pl.ds(pl.multiple_of(j * tile, tile), tile)
        gate_proj = nn_dot(x_ref[...], gate_ref[slot])
        up_proj = nn_dot(x_ref[...], up_ref[slot])
        if not last:
            active_ref[:, column] = gate_proj
            turn_ref[:, column] = up_proj
            return
        gate_proj = gate_proj + before[0][:, column]
        up_proj = up_proj + before[1][:, column]
        sig = jax.nn.sigmoid(gate_proj)
        active = gate_proj * sig
        hid_ref[:, column] = (active * up_proj).astype(BF)
        active_ref[:, column] = active
        turn_ref[:, column] = up_proj * (sig * (1.0 + gate_proj * (1.0 - sig)))

    streamed(gate_hbm.shape[1] // tile, gate_ref.shape[0], copies, body, first)


def enter(own, other, gate, up, *before):
    half, width = own.shape
    units = gate.shape[1]
    rows = 2 * half
    tile = tile_of(units, (256, 128))
    depth = min(DEPTH, units // tile)
    last = len(before) > 0
    wide = shape((rows, units), F32)
    outs = [shape((rows, units)), wide, wide] if last else [wide, wide]
    return pl.pallas_call(
        lambda *refs: enter_kernel(tile, last, *refs),
        in_specs=[VMEM, VMEM, HBM, HBM] + [VMEM] * len(before),
        out_specs=[VMEM] * len(outs),
        out_shape=outs,
        scratch_shapes=[
            pltpu.VMEM((rows, width), BF),
            pltpu.VMEM((depth, width, tile), BF),
            pltpu.VMEM((depth, width, tile), BF),
            pltpu.SemaphoreType.DMA((2, depth)),
        ],
        compiler_params=grant((rows, width, BF), (2 * depth * tile, width, BF), least=46 * MIB),
        cost_estimate=cost(4 * rows * width * units, 4 * width * units),
        name="enter",
    )(own, other, gate, up, *before)


def turn_kernel(tile, ca_ref, cb_ref, down_hbm, active_ref, factor_ref, gb_ref, ub_ref,
                c_ref, down_ref, sems):
    half = ca_ref.shape[0]

    def first():
        c_ref[:half] = ca_ref[...]
        c_ref[half:] = cb_ref[...]

    def copies(j, slot):
        row = pl.ds(pl.multiple_of(j * tile, tile), tile)
        return (pltpu.make_async_copy(down_hbm.at[row, :], down_ref.at[slot], sems.at[slot]),)

    def body(j, slot):
        span = pl.ds(pl.multiple_of(j * tile, tile), tile)
        back = nt_dot(c_ref[...], down_ref[slot])
        gb_ref[:, span] = (back * factor_ref[:, span]).astype(BF)
        ub_ref[:, span] = (back * active_ref[:, span]).astype(BF)

    streamed(down_hbm.shape[0] // tile, down_ref.shape[0], copies, body, first)


def turn(own, other, down, active, factor):
    half, width = own.shape
    units = down.shape[0]
    rows = 2 * half
    tile = tile_of(units, (256, 128))
    depth = min(DEPTH, units // tile)
    return pl.pallas_call(
        lambda *refs: turn_kernel(tile, *refs),
        in_specs=[VMEM, VMEM, HBM, VMEM, VMEM],
        out_specs=[VMEM] * 2,
        out_shape=[shape((rows, units))] * 2,
        scratch_shapes=[
            pltpu.VMEM((rows, width), BF),
            pltpu.VMEM((depth, tile, width), BF),
            pltpu.SemaphoreType.DMA((depth,)),
        ],
        compiler_params=grant((rows, width, BF), (depth * tile, width, BF), least=46 * MIB),
        cost_estimate=cost(2 * rows * width * units, 2 * width * units),
        name="turn",
    )(own, other, down, active, factor)


def leave_kernel(step, hid_ref, gb_ref, ub_ref, gate_hbm, up_hbm, down_hbm, own_ref, other_ref,
                 gate_ref, up_ref, down_ref, sems):
    half = own_ref.shape[1]

    def copies(j, slot):
        span = pl.ds(pl.multiple_of(j * step, step), step)
        return (
            pltpu.make_async_copy(down_hbm.at[:, span], down_ref.at[slot], sems.at[0, slot]),
            pltpu.make_async_copy(gate_hbm.at[span, :], gate_ref.at[slot], sems.at[1, slot]),
            pltpu.make_async_copy(up_hbm.at[span, :], up_ref.at[slot], sems.at[2, slot]),
        )

    def body(j, slot):
        span = pl.ds(pl.multiple_of(j * step, step), step)
        result = nn_dot(hid_ref[...], down_ref[slot]).astype(BF)
        own_ref[0, :, span] = result[:half]
        other_ref[0, :, span] = result[half:]
        result = nt_dot(gb_ref[...], gate_ref[slot]) + nt_dot(ub_ref[...], up_ref[slot])
        result = result.astype(BF)
        own_ref[1, :, span] = result[:half]
        other_ref[1, :, span] = result[half:]

    streamed(gate_hbm.shape[0] // step, gate_ref.shape[0], copies, body, lambda: None)


def leave(hid, gb, ub, gate, up, down):
    rows, units = gb.shape
    width = gate.shape[0]
    half = rows // 2
    step = tile_of(width, (512, 256, 128))
    depth = min(DEPTH, width // step)
    return pl.pallas_call(
        lambda *refs: leave_kernel(step, *refs),
        in_specs=[VMEM] * 3 + [HBM] * 3,
        out_specs=[VMEM] * 2,
        out_shape=[shape((2, half, width))] * 2,
        scratch_shapes=[
            pltpu.VMEM((depth, step, units), BF),
            pltpu.VMEM((depth, step, units), BF),
            pltpu.VMEM((depth, units, step), BF),
            pltpu.SemaphoreType.DMA((3, depth)),
        ],
        compiler_params=grant((3 * depth * step, units, BF), least=40 * MIB),
        cost_estimate=cost(6 * rows * width * units, 6 * width * units),
        name="leave",
    )(hid, gb, ub, gate, up, down)


def fold_kernel(first_ref, own_ref, mate_ref, *chunks):
    count = chunks[0].shape[1]
    ring = own_ref.shape[1] // count
    for k in range(ring):
        span = slice(k * count, (k + 1) * count)
        both = own_ref[:, span].astype(F32) + mate_ref[:, span].astype(F32)
        chunks[k][...] = both.astype(BF)
    if len(chunks) > ring:
        @pl.when(first_ref[0] == 1)
        def _():
            chunks[ring][...] = chunks[1][...]

        @pl.when(first_ref[0] != 1)
        def _():
            chunks[ring][...] = chunks[ring - 1][...]


def fold(first, own, mate, ring, chunks):
    sides, rows, width = own.shape
    return pl.pallas_call(
        fold_kernel,
        in_specs=[pl.BlockSpec(memory_space=pltpu.SMEM), VMEM, VMEM],
        out_specs=[VMEM] * chunks,
        out_shape=[shape((sides, rows // ring, width))] * chunks,
        compiler_params=grant(),
        cost_estimate=cost(own.size, 6 * own.size),
        name="fold",
    )(first, own, mate)


def rows_dot(left, right):
    return lax.dot_general(
        left, right, (((0,), (0,)), ((), ())), preferred_element_type=F32
    ).astype(BF)


def on_device(tokens, modality, gate, up, down, out_grad):
    _, width = out_grad.shape
    groups = lax.axis_size("seq")
    ring = lax.axis_size("dp") // CORES
    part = width // groups
    seat = lax.axis_index("seq").reshape(1)
    first = (lax.axis_index("dp") < CORES).astype(jnp.int32).reshape(1)
    tokens, modality, first, seat = lax.optimization_barrier((tokens, modality, first, seat))

    def shift(value, k):
        return lax.ppermute(value, "dp", [
            (z * CORES + c, (z + k) % ring * CORES + c) for z in range(ring) for c in range(CORES)])

    def swap(value):
        return lax.ppermute(value, "dp", [
            (z * CORES + c, z * CORES + 1 - c) for z in range(ring) for c in range(CORES)])

    def across(value, mask):
        return lax.ppermute(value, "seq", [(g, g ^ mask) for g in range(groups)])

    def gathered(block):
        return jnp.concatenate([block] + [shift(block, k) for k in range(1, ring)], axis=0)

    def slices_of(blocks):
        small = jnp.stack([blocks[0]] + [across(blocks[m], m) for m in range(1, groups)])
        pieces = [small] + [shift(small, k) for k in range(1, ring)]
        own = jnp.stack(pieces, axis=1)
        mate = swap(own)
        both_cores = jnp.stack([own, mate], axis=1)
        return (both_cores[..., :part].reshape(-1, part), both_cores[..., part:].reshape(-1, part))

    def near(value):
        held = [[value]] + [None] * (groups - 1)
        for m in range(1, groups):
            if m & (m - 1) == 0:
                held[m] = [across(value, m)]
        return held

    def relay(held):
        half = held[0][0].shape[0] // 2
        held = list(held)
        for m in range(1, groups):
            low, high = m & -m, 1 << (m.bit_length() - 1)
            if low != high:
                a = jnp.concatenate(held[m ^ low], axis=0)
                b = jnp.concatenate(held[m ^ high], axis=0)
                held[m] = [across(a[:half], low), across(b[half:], high)]
        return held

    def after(values, others):
        leaves, tree = jax.tree.flatten(values)
        return jax.tree.unflatten(
            tree, lax.optimization_barrier((*leaves, *others))[:len(leaves)])

    def returned(own, mate):
        line = ring == 4
        sums = fold(first, own, mate, ring, ring + line)
        if not line:
            return [sums[0]] + [shift(sums[k], -k) for k in range(1, ring)]

        def along(value, pairs):
            return lax.ppermute(value, "dp", [
                (a * CORES + c, b * CORES + c) for a, b in pairs for c in range(CORES)])

        far = along(sums[4], [(0, 1), (3, 2)])
        terms = [along(sums[1], [(1, 0), (2, 1), (3, 2)]),
                 along(sums[3], [(0, 1), (1, 2), (2, 3)])]
        mid = (sums[2].astype(F32) + far.astype(F32)).astype(BF)
        return [sums[0], *terms, shift(mid, 2)]

    def stack(held):
        return jnp.concatenate(sum(held, []), axis=0)

    left, right, *blocks = pick(seat, modality, tokens, out_grad, groups)
    tok = [gathered(side) for side in (left, right)]
    tok_mate = []
    for side in tok:
        tok_mate.append(swap(side))
    tok_all, cot_all = slices_of(blocks)
    cot = gathered(out_grad)
    cot_mate = swap(cot)
    before = enter(tok[0], tok_mate[0], gate, up)
    hid, active, factor = enter(tok[1], tok_mate[1], gate, up, *before)
    all_hid = relay(near(hid))
    gb, ub = turn(cot, cot_mate, down, active, factor)
    all_gb = near(gb)
    all_ub = near(ub)
    own, other = leave(hid, gb, ub, gate, up, down)

    mate = swap(other)
    terms = returned(own, mate)
    all_hid = after(all_hid, terms[:1])
    all_gb = relay(all_gb)
    all_ub = relay(after(all_ub, terms[:1]))
    down_grad = rows_dot(stack(all_hid), cot_all)
    gate_grad = rows_dot(tok_all, stack(all_gb))
    up_grad = rows_dot(tok_all, stack(all_ub))
    terms = after(terms, [up_grad])

    def total(side):
        value = terms[0][side].astype(F32)
        for term in terms[1:]:
            value = value + term[side].astype(F32)
        return value.astype(BF)

    output, in_grad = total(0), total(1)
    return output, in_grad, gate_grad, up_grad, down_grad


def solution(mesh):
    rows = P(("dp", "seq"), None)
    return jax.shard_map(
        on_device,
        mesh=mesh,
        in_specs=(rows, P(("dp", "seq")), P(None, "dp"), P(None, "dp"), P("dp", None), rows),
        out_specs=(rows, rows, P("seq", "dp"), P("seq", "dp"), P("dp", "seq")),
        check_vma=False,
    )
```

```python
import jax
import jax.numpy as jnp
from jax import lax
from jax.experimental import pallas as pl
from jax.experimental.pallas import tpu as pltpu
from jax.sharding import PartitionSpec as P


BF = jnp.bfloat16
F32 = jnp.float32
CORES = 2
MIB = 1 << 20
ALL_VMEM = 67043328


HBM = pl.BlockSpec(memory_space=pltpu.HBM)
VMEM = pl.BlockSpec(memory_space=pltpu.VMEM)


def tile_of(extent, options):
    for option in options:
        if extent % option == 0:
            return option
    return extent


def cost(flops, nbytes):
    return pl.CostEstimate(flops=flops, bytes_accessed=nbytes, transcendentals=0)


def shape(dims, dtype=BF):
    return jax.ShapeDtypeStruct(dims, dtype)


def grant(*arrays, least=0):
    total = sum(2 * r * c if d == BF else 4 * r * c for r, c, d in arrays)
    return pltpu.CompilerParams(vmem_limit_bytes=min(max(total + 6 * MIB, least), ALL_VMEM))


def nt_dot(left, right):
    return lax.dot_general(left, right, (((1,), (1,)), ((), ())), preferred_element_type=F32)


def nn_dot(left, right):
    return jnp.dot(left, right, preferred_element_type=F32)


def pick_kernel(seat_ref, flag_ref, tokens_ref, cot_ref, left_ref, right_ref, *refs):
    blocks, picked_ref = refs[:-1], refs[-1]
    rows = cot_ref.shape[0]
    count = tokens_ref.shape[0]
    flags = (flag_ref[...] == 1).astype(F32)
    before = lax.broadcasted_iota(jnp.int32, (count, count), 0)
    after = lax.broadcasted_iota(jnp.int32, (count, count), 1)
    ranks = nn_dot(flags, (before <= after).astype(F32))
    slots = lax.broadcasted_iota(jnp.int32, (rows, count), 0).astype(F32) + 1.0
    chosen = (jnp.broadcast_to(ranks, (rows, count)) == slots) & (
        jnp.broadcast_to(flags, (rows, count)) == 1.0
    )
    picked_ref[...] = nn_dot(chosen.astype(BF), tokens_ref[...]).astype(BF)
    middle = left_ref.shape[1]
    left_ref[...] = picked_ref[:, :middle]
    right_ref[...] = picked_ref[:, middle:]
    part = picked_ref.shape[1] // len(blocks)
    for m, block in enumerate(blocks):
        span = pl.ds(pl.multiple_of((seat_ref[0] ^ m) * part, part), part)
        block[:, :part] = picked_ref[:, span]
        block[:, part:] = cot_ref[:, span]


def pick(seat, modality, tokens, out_grad, groups):
    rows, width = out_grad.shape
    half, block = shape((rows, width // 2)), shape((rows, 2 * width // groups))
    return pl.pallas_call(
        pick_kernel,
        in_specs=[pl.BlockSpec(memory_space=pltpu.SMEM)] + [VMEM] * 3,
        out_specs=[VMEM] * (2 + groups),
        out_shape=[half, half] + [block] * groups,
        scratch_shapes=[pltpu.VMEM((rows, width), BF)],
        compiler_params=grant(),
        name="pick",
    )(seat, modality.reshape(1, -1), tokens, out_grad)


def streamed(steps, depth, copies, body, first):
    depth = min(depth, steps)

    def start(j):
        for copy in copies(j, lax.rem(j, depth)):
            copy.start()

    for j in range(depth):
        start(jnp.int32(j))
    first()

    @pl.loop(0, steps)
    def _(j):
        slot = lax.rem(j, depth)
        for copy in copies(j, slot):
            copy.wait()
        body(j, slot)

        @pl.when(j + depth < steps)
        def _():
            start(j + depth)


DEPTH = 5


def enter_kernel(tile, last, xa_ref, xb_ref, gate_hbm, up_hbm, *refs):
    (*before, hid_ref, active_ref, turn_ref) = refs[:5] if last else (None, *refs[:2])
    x_ref, gate_ref, up_ref, sems = refs[5:] if last else refs[2:]
    half, depth = xa_ref.shape
    rows = pl.ds(depth if last else 0, depth)

    def first():
        x_ref[:half] = xa_ref[...]
        x_ref[half:] = xb_ref[...]

    def copies(j, slot):
        column = pl.ds(pl.multiple_of(j * tile, tile), tile)
        return (
            pltpu.make_async_copy(gate_hbm.at[rows, column], gate_ref.at[slot], sems.at[0, slot]),
            pltpu.make_async_copy(up_hbm.at[rows, column], up_ref.at[slot], sems.at[1, slot]),
        )

    def body(j, slot):
        column = pl.ds(pl.multiple_of(j * tile, tile), tile)
        gate_proj = nn_dot(x_ref[...], gate_ref[slot])
        up_proj = nn_dot(x_ref[...], up_ref[slot])
        if not last:
            active_ref[:, column] = gate_proj
            turn_ref[:, column] = up_proj
            return
        gate_proj = gate_proj + before[0][:, column]
        up_proj = up_proj + before[1][:, column]
        sig = jax.nn.sigmoid(gate_proj)
        active = gate_proj * sig
        hid_ref[:, column] = (active * up_proj).astype(BF)
        active_ref[:, column] = active
        turn_ref[:, column] = up_proj * (sig * (1.0 + gate_proj * (1.0 - sig)))

    streamed(gate_hbm.shape[1] // tile, gate_ref.shape[0], copies, body, first)


def enter(own, other, gate, up, *before):
    half, width = own.shape
    units = gate.shape[1]
    rows = 2 * half
    tile = tile_of(units, (256, 128))
    depth = min(DEPTH, units // tile)
    last = len(before) > 0
    wide = shape((rows, units), F32)
    outs = [shape((rows, units)), wide, wide] if last else [wide, wide]
    return pl.pallas_call(
        lambda *refs: enter_kernel(tile, last, *refs),
        in_specs=[VMEM, VMEM, HBM, HBM] + [VMEM] * len(before),
        out_specs=[VMEM] * len(outs),
        out_shape=outs,
        scratch_shapes=[
            pltpu.VMEM((rows, width), BF),
            pltpu.VMEM((depth, width, tile), BF),
            pltpu.VMEM((depth, width, tile), BF),
            pltpu.SemaphoreType.DMA((2, depth)),
        ],
        compiler_params=grant((rows, width, BF), (2 * depth * tile, width, BF), least=46 * MIB),
        cost_estimate=cost(4 * rows * width * units, 4 * width * units),
        name="enter",
    )(own, other, gate, up, *before)


def turn_kernel(tile, ca_ref, cb_ref, down_hbm, active_ref, factor_ref, gb_ref, ub_ref,
                c_ref, down_ref, sems):
    half = ca_ref.shape[0]

    def first():
        c_ref[:half] = ca_ref[...]
        c_ref[half:] = cb_ref[...]

    def copies(j, slot):
        row = pl.ds(pl.multiple_of(j * tile, tile), tile)
        return (pltpu.make_async_copy(down_hbm.at[row, :], down_ref.at[slot], sems.at[slot]),)

    def body(j, slot):
        span = pl.ds(pl.multiple_of(j * tile, tile), tile)
        back = nt_dot(c_ref[...], down_ref[slot])
        gb_ref[:, span] = (back * factor_ref[:, span]).astype(BF)
        ub_ref[:, span] = (back * active_ref[:, span]).astype(BF)

    streamed(down_hbm.shape[0] // tile, down_ref.shape[0], copies, body, first)


def turn(own, other, down, active, factor):
    half, width = own.shape
    units = down.shape[0]
    rows = 2 * half
    tile = tile_of(units, (256, 128))
    depth = min(DEPTH, units // tile)
    return pl.pallas_call(
        lambda *refs: turn_kernel(tile, *refs),
        in_specs=[VMEM, VMEM, HBM, VMEM, VMEM],
        out_specs=[VMEM] * 2,
        out_shape=[shape((rows, units))] * 2,
        scratch_shapes=[
            pltpu.VMEM((rows, width), BF),
            pltpu.VMEM((depth, tile, width), BF),
            pltpu.SemaphoreType.DMA((depth,)),
        ],
        compiler_params=grant((rows, width, BF), (depth * tile, width, BF), least=46 * MIB),
        cost_estimate=cost(2 * rows * width * units, 2 * width * units),
        name="turn",
    )(own, other, down, active, factor)


def leave_kernel(step, hid_ref, gb_ref, ub_ref, gate_hbm, up_hbm, down_hbm, own_ref, other_ref,
                 gate_ref, up_ref, down_ref, sems):
    half = own_ref.shape[1]

    def copies(j, slot):
        span = pl.ds(pl.multiple_of(j * step, step), step)
        return (
            pltpu.make_async_copy(down_hbm.at[:, span], down_ref.at[slot], sems.at[0, slot]),
            pltpu.make_async_copy(gate_hbm.at[span, :], gate_ref.at[slot], sems.at[1, slot]),
            pltpu.make_async_copy(up_hbm.at[span, :], up_ref.at[slot], sems.at[2, slot]),
        )

    def body(j, slot):
        span = pl.ds(pl.multiple_of(j * step, step), step)
        result = nn_dot(hid_ref[...], down_ref[slot]).astype(BF)
        own_ref[0, :, span] = result[:half]
        other_ref[0, :, span] = result[half:]
        result = nt_dot(gb_ref[...], gate_ref[slot]) + nt_dot(ub_ref[...], up_ref[slot])
        result = result.astype(BF)
        own_ref[1, :, span] = result[:half]
        other_ref[1, :, span] = result[half:]

    streamed(gate_hbm.shape[0] // step, gate_ref.shape[0], copies, body, lambda: None)


def leave(hid, gb, ub, gate, up, down):
    rows, units = gb.shape
    width = gate.shape[0]
    half = rows // 2
    step = tile_of(width, (512, 256, 128))
    depth = min(DEPTH, width // step)
    return pl.pallas_call(
        lambda *refs: leave_kernel(step, *refs),
        in_specs=[VMEM] * 3 + [HBM] * 3,
        out_specs=[VMEM] * 2,
        out_shape=[shape((2, half, width))] * 2,
        scratch_shapes=[
            pltpu.VMEM((depth, step, units), BF),
            pltpu.VMEM((depth, step, units), BF),
            pltpu.VMEM((depth, units, step), BF),
            pltpu.SemaphoreType.DMA((3, depth)),
        ],
        compiler_params=grant((3 * depth * step, units, BF), least=40 * MIB),
        cost_estimate=cost(6 * rows * width * units, 6 * width * units),
        name="leave",
    )(hid, gb, ub, gate, up, down)


def fold_kernel(first_ref, own_ref, mate_ref, *chunks):
    count = chunks[0].shape[1]
    ring = own_ref.shape[1] // count
    for k in range(ring):
        span = slice(k * count, (k + 1) * count)
        both = own_ref[:, span].astype(F32) + mate_ref[:, span].astype(F32)
        chunks[k][...] = both.astype(BF)
    if len(chunks) > ring:
        @pl.when(first_ref[0] == 1)
        def _():
            chunks[ring][...] = chunks[1][...]

        @pl.when(first_ref[0] != 1)
        def _():
            chunks[ring][...] = chunks[ring - 1][...]


def fold(first, own, mate, ring, chunks):
    sides, rows, width = own.shape
    return pl.pallas_call(
        fold_kernel,
        in_specs=[pl.BlockSpec(memory_space=pltpu.SMEM), VMEM, VMEM],
        out_specs=[VMEM] * chunks,
        out_shape=[shape((sides, rows // ring, width))] * chunks,
        compiler_params=grant(),
        cost_estimate=cost(own.size, 6 * own.size),
        name="fold",
    )(first, own, mate)


def rows_dot(left, right):
    return lax.dot_general(
        left, right, (((0,), (0,)), ((), ())), preferred_element_type=F32
    ).astype(BF)


def on_device(tokens, modality, gate, up, down, out_grad):
    _, width = out_grad.shape
    groups = lax.axis_size("seq")
    ring = lax.axis_size("dp") // CORES
    part = width // groups
    seat = lax.axis_index("seq").reshape(1)
    first = (lax.axis_index("dp") < CORES).astype(jnp.int32).reshape(1)
    tokens, modality, first, seat = lax.optimization_barrier((tokens, modality, first, seat))

    def shift(value, k):
        return lax.ppermute(value, "dp", [
            (z * CORES + c, (z + k) % ring * CORES + c) for z in range(ring) for c in range(CORES)])

    def swap(value):
        return lax.ppermute(value, "dp", [
            (z * CORES + c, z * CORES + 1 - c) for z in range(ring) for c in range(CORES)])

    def across(value, mask):
        return lax.ppermute(value, "seq", [(g, g ^ mask) for g in range(groups)])

    def gathered(block):
        return jnp.concatenate([block] + [shift(block, k) for k in range(1, ring)], axis=0)

    def slices_of(blocks):
        small = jnp.stack([blocks[0]] + [across(blocks[m], m) for m in range(1, groups)])
        pieces = [small] + [shift(small, k) for k in range(1, ring)]
        own = jnp.stack(pieces, axis=1)
        mate = swap(own)
        both_cores = jnp.stack([own, mate], axis=1)
        return (both_cores[..., :part].reshape(-1, part), both_cores[..., part:].reshape(-1, part))

    def near(value):
        held = [[value]] + [None] * (groups - 1)
        for m in range(1, groups):
            if m & (m - 1) == 0:
                held[m] = [across(value, m)]
        return held

    def relay(held):
        half = held[0][0].shape[0] // 2
        held = list(held)
        for m in range(1, groups):
            low, high = m & -m, 1 << (m.bit_length() - 1)
            if low != high:
                a = jnp.concatenate(held[m ^ low], axis=0)
                b = jnp.concatenate(held[m ^ high], axis=0)
                held[m] = [across(a[:half], low), across(b[half:], high)]
        return held

    def after(values, others):
        leaves, tree = jax.tree.flatten(values)
        return jax.tree.unflatten(
            tree, lax.optimization_barrier((*leaves, *others))[:len(leaves)])

    def returned(own, mate):
        line = ring == 4
        sums = fold(first, own, mate, ring, ring + line)
        if not line:
            return [sums[0]] + [shift(sums[k], -k) for k in range(1, ring)], sums[0]

        def along(value, pairs):
            return lax.ppermute(value, "dp", [
                (a * CORES + c, b * CORES + c) for a, b in pairs for c in range(CORES)])

        far = along(sums[4], [(0, 1), (3, 2)])
        terms = [along(sums[1], [(1, 0), (2, 1), (3, 2)]),
                 along(sums[3], [(0, 1), (1, 2), (2, 3)])]
        mid = (sums[2].astype(F32) + far.astype(F32)).astype(BF)
        return [sums[0], *terms, shift(mid, 2)], mid

    def stack(held):
        return jnp.concatenate(sum(held, []), axis=0)

    left, right, *blocks = pick(seat, modality, tokens, out_grad, groups)
    tok = [gathered(side) for side in (left, right)]
    tok_mate = []
    for side in tok:
        tok_mate.append(swap(side))
    tok_all, cot_all = slices_of(blocks)
    cot = gathered(out_grad)
    cot_mate = swap(cot)
    before = enter(tok[0], tok_mate[0], gate, up)
    hid, active, factor = enter(tok[1], tok_mate[1], gate, up, *before)
    all_hid = relay(near(hid))
    gb, ub = turn(cot, cot_mate, down, active, factor)
    all_gb = near(gb)
    all_ub = near(ub)
    own, other = leave(hid, gb, ub, gate, up, down)

    mate = swap(other)
    terms, last = returned(own, mate)
    all_hid = after(all_hid, terms[:1])
    all_gb = relay(all_gb)
    all_ub = relay(after(all_ub, [last]))
    down_grad = rows_dot(stack(all_hid), cot_all)
    gate_grad = rows_dot(tok_all, stack(all_gb))
    up_grad = rows_dot(tok_all, stack(all_ub))
    terms = after(terms, [up_grad])

    def total(side):
        value = terms[0][side].astype(F32)
        for term in terms[1:]:
            value = value + term[side].astype(F32)
        return value.astype(BF)

    output, in_grad = total(0), total(1)
    return output, in_grad, gate_grad, up_grad, down_grad


def solution(mesh):
    rows = P(("dp", "seq"), None)
    return jax.shard_map(
        on_device,
        mesh=mesh,
        in_specs=(rows, P(("dp", "seq")), P(None, "dp"), P(None, "dp"), P("dp", None), rows),
        out_specs=(rows, rows, P("seq", "dp"), P("seq", "dp"), P("dp", "seq")),
        check_vma=False,
    )
```

```python
import jax
import jax.numpy as jnp
from jax import lax
from jax.experimental import pallas as pl
from jax.experimental.pallas import tpu as pltpu
from jax.sharding import PartitionSpec as P


BF = jnp.bfloat16
F32 = jnp.float32
CORES = 2
MIB = 1 << 20
ALL_VMEM = 67043328


HBM = pl.BlockSpec(memory_space=pltpu.HBM)
VMEM = pl.BlockSpec(memory_space=pltpu.VMEM)


def tile_of(extent, options):
    for option in options:
        if extent % option == 0:
            return option
    return extent


def cost(flops, nbytes):
    return pl.CostEstimate(flops=flops, bytes_accessed=nbytes, transcendentals=0)


def shape(dims, dtype=BF):
    return jax.ShapeDtypeStruct(dims, dtype)


def grant(*arrays, least=0):
    total = sum(2 * r * c if d == BF else 4 * r * c for r, c, d in arrays)
    return pltpu.CompilerParams(vmem_limit_bytes=min(max(total + 6 * MIB, least), ALL_VMEM))


def nt_dot(left, right):
    return lax.dot_general(left, right, (((1,), (1,)), ((), ())), preferred_element_type=F32)


def nn_dot(left, right):
    return jnp.dot(left, right, preferred_element_type=F32)


def pick_kernel(seat_ref, flag_ref, tokens_ref, cot_ref, left_ref, right_ref, *refs):
    blocks, picked_ref = refs[:-1], refs[-1]
    rows = cot_ref.shape[0]
    count = tokens_ref.shape[0]
    flags = (flag_ref[...] == 1).astype(F32)
    before = lax.broadcasted_iota(jnp.int32, (count, count), 0)
    after = lax.broadcasted_iota(jnp.int32, (count, count), 1)
    ranks = nn_dot(flags, (before <= after).astype(F32))
    slots = lax.broadcasted_iota(jnp.int32, (rows, count), 0).astype(F32) + 1.0
    chosen = (jnp.broadcast_to(ranks, (rows, count)) == slots) & (
        jnp.broadcast_to(flags, (rows, count)) == 1.0
    )
    picked_ref[...] = nn_dot(chosen.astype(BF), tokens_ref[...]).astype(BF)
    middle = left_ref.shape[1]
    left_ref[...] = picked_ref[:, :middle]
    right_ref[...] = picked_ref[:, middle:]
    part = picked_ref.shape[1] // len(blocks)
    for m, block in enumerate(blocks):
        span = pl.ds(pl.multiple_of((seat_ref[0] ^ m) * part, part), part)
        block[:, :part] = picked_ref[:, span]
        block[:, part:] = cot_ref[:, span]


def pick(seat, modality, tokens, out_grad, groups):
    rows, width = out_grad.shape
    half, block = shape((rows, width // 2)), shape((rows, 2 * width // groups))
    return pl.pallas_call(
        pick_kernel,
        in_specs=[pl.BlockSpec(memory_space=pltpu.SMEM)] + [VMEM] * 3,
        out_specs=[VMEM] * (2 + groups),
        out_shape=[half, half] + [block] * groups,
        scratch_shapes=[pltpu.VMEM((rows, width), BF)],
        compiler_params=grant(),
        name="pick",
    )(seat, modality.reshape(1, -1), tokens, out_grad)


def streamed(steps, depth, copies, body, first):
    depth = min(depth, steps)

    def start(j):
        for copy in copies(j, lax.rem(j, depth)):
            copy.start()

    for j in range(depth):
        start(jnp.int32(j))
    first()

    @pl.loop(0, steps)
    def _(j):
        slot = lax.rem(j, depth)
        for copy in copies(j, slot):
            copy.wait()
        body(j, slot)

        @pl.when(j + depth < steps)
        def _():
            start(j + depth)


DEPTH = 5


def enter_kernel(tile, last, xa_ref, xb_ref, gate_hbm, up_hbm, *refs):
    (*before, hid_ref, active_ref, turn_ref) = refs[:5] if last else (None, *refs[:2])
    x_ref, gate_ref, up_ref, sems = refs[5:] if last else refs[2:]
    half, depth = xa_ref.shape
    rows = pl.ds(depth if last else 0, depth)

    def first():
        x_ref[:half] = xa_ref[...]
        x_ref[half:] = xb_ref[...]

    def copies(j, slot):
        column = pl.ds(pl.multiple_of(j * tile, tile), tile)
        return (
            pltpu.make_async_copy(gate_hbm.at[rows, column], gate_ref.at[slot], sems.at[0, slot]),
            pltpu.make_async_copy(up_hbm.at[rows, column], up_ref.at[slot], sems.at[1, slot]),
        )

    def body(j, slot):
        column = pl.ds(pl.multiple_of(j * tile, tile), tile)
        gate_proj = nn_dot(x_ref[...], gate_ref[slot])
        up_proj = nn_dot(x_ref[...], up_ref[slot])
        if not last:
            active_ref[:, column] = gate_proj
            turn_ref[:, column] = up_proj
            return
        gate_proj = gate_proj + before[0][:, column]
        up_proj = up_proj + before[1][:, column]
        sig = jax.nn.sigmoid(gate_proj)
        active = gate_proj * sig
        hid_ref[:, column] = (active * up_proj).astype(BF)
        active_ref[:, column] = active
        turn_ref[:, column] = up_proj * (sig * (1.0 + gate_proj * (1.0 - sig)))

    streamed(gate_hbm.shape[1] // tile, gate_ref.shape[0], copies, body, first)


def enter(own, other, gate, up, *before):
    half, width = own.shape
    units = gate.shape[1]
    rows = 2 * half
    tile = tile_of(units, (256, 128))
    depth = min(DEPTH, units // tile)
    last = len(before) > 0
    wide = shape((rows, units), F32)
    outs = [shape((rows, units)), wide, wide] if last else [wide, wide]
    return pl.pallas_call(
        lambda *refs: enter_kernel(tile, last, *refs),
        in_specs=[VMEM, VMEM, HBM, HBM] + [VMEM] * len(before),
        out_specs=[VMEM] * len(outs),
        out_shape=outs,
        scratch_shapes=[
            pltpu.VMEM((rows, width), BF),
            pltpu.VMEM((depth, width, tile), BF),
            pltpu.VMEM((depth, width, tile), BF),
            pltpu.SemaphoreType.DMA((2, depth)),
        ],
        compiler_params=grant((rows, width, BF), (2 * depth * tile, width, BF), least=46 * MIB),
        cost_estimate=cost(4 * rows * width * units, 4 * width * units),
        name="enter",
    )(own, other, gate, up, *before)


def turn_kernel(tile, ca_ref, cb_ref, down_hbm, active_ref, factor_ref, both_ref,
                c_ref, down_ref, sems):
    half = ca_ref.shape[0]

    def first():
        c_ref[:half] = ca_ref[...]
        c_ref[half:] = cb_ref[...]

    def copies(j, slot):
        row = pl.ds(pl.multiple_of(j * tile, tile), tile)
        return (pltpu.make_async_copy(down_hbm.at[row, :], down_ref.at[slot], sems.at[slot]),)

    def body(j, slot):
        span = pl.ds(pl.multiple_of(j * tile, tile), tile)
        back = nt_dot(c_ref[...], down_ref[slot])
        both_ref[0, :, span] = (back * factor_ref[:, span]).astype(BF)
        both_ref[1, :, span] = (back * active_ref[:, span]).astype(BF)

    streamed(down_hbm.shape[0] // tile, down_ref.shape[0], copies, body, first)


def turn(own, other, down, active, factor):
    half, width = own.shape
    units = down.shape[0]
    rows = 2 * half
    tile = tile_of(units, (256, 128))
    depth = min(DEPTH, units // tile)
    return pl.pallas_call(
        lambda *refs: turn_kernel(tile, *refs),
        in_specs=[VMEM, VMEM, HBM, VMEM, VMEM],
        out_specs=VMEM,
        out_shape=shape((2, rows, units)),
        scratch_shapes=[
            pltpu.VMEM((rows, width), BF),
            pltpu.VMEM((depth, tile, width), BF),
            pltpu.SemaphoreType.DMA((depth,)),
        ],
        compiler_params=grant((rows, width, BF), (depth * tile, width, BF), least=46 * MIB),
        cost_estimate=cost(2 * rows * width * units, 2 * width * units),
        name="turn",
    )(own, other, down, active, factor)


def leave_kernel(step, hid_ref, both_ref, gate_hbm, up_hbm, down_hbm, own_ref, other_ref,
                 gate_ref, up_ref, down_ref, sems):
    half = own_ref.shape[1]

    def copies(j, slot):
        span = pl.ds(pl.multiple_of(j * step, step), step)
        return (
            pltpu.make_async_copy(down_hbm.at[:, span], down_ref.at[slot], sems.at[0, slot]),
            pltpu.make_async_copy(gate_hbm.at[span, :], gate_ref.at[slot], sems.at[1, slot]),
            pltpu.make_async_copy(up_hbm.at[span, :], up_ref.at[slot], sems.at[2, slot]),
        )

    def body(j, slot):
        span = pl.ds(pl.multiple_of(j * step, step), step)
        result = nn_dot(hid_ref[...], down_ref[slot]).astype(BF)
        own_ref[0, :, span] = result[:half]
        other_ref[0, :, span] = result[half:]
        result = nt_dot(both_ref[0], gate_ref[slot]) + nt_dot(both_ref[1], up_ref[slot])
        result = result.astype(BF)
        own_ref[1, :, span] = result[:half]
        other_ref[1, :, span] = result[half:]

    streamed(gate_hbm.shape[0] // step, gate_ref.shape[0], copies, body, lambda: None)


def leave(hid, both, gate, up, down):
    rows, units = hid.shape
    width = gate.shape[0]
    half = rows // 2
    step = tile_of(width, (512, 256, 128))
    depth = min(DEPTH, width // step)
    return pl.pallas_call(
        lambda *refs: leave_kernel(step, *refs),
        in_specs=[VMEM] * 2 + [HBM] * 3,
        out_specs=[VMEM] * 2,
        out_shape=[shape((2, half, width))] * 2,
        scratch_shapes=[
            pltpu.VMEM((depth, step, units), BF),
            pltpu.VMEM((depth, step, units), BF),
            pltpu.VMEM((depth, units, step), BF),
            pltpu.SemaphoreType.DMA((3, depth)),
        ],
        compiler_params=grant((3 * depth * step, units, BF), least=40 * MIB),
        cost_estimate=cost(6 * rows * width * units, 6 * width * units),
        name="leave",
    )(hid, both, gate, up, down)


def fold_kernel(first_ref, own_ref, mate_ref, *chunks):
    count = chunks[0].shape[1]
    ring = own_ref.shape[1] // count
    for k in range(ring):
        span = slice(k * count, (k + 1) * count)
        both = own_ref[:, span].astype(F32) + mate_ref[:, span].astype(F32)
        chunks[k][...] = both.astype(BF)
    if len(chunks) > ring:
        @pl.when(first_ref[0] == 1)
        def _():
            chunks[ring][...] = chunks[1][...]

        @pl.when(first_ref[0] != 1)
        def _():
            chunks[ring][...] = chunks[ring - 1][...]


def fold(first, own, mate, ring, chunks):
    sides, rows, width = own.shape
    return pl.pallas_call(
        fold_kernel,
        in_specs=[pl.BlockSpec(memory_space=pltpu.SMEM), VMEM, VMEM],
        out_specs=[VMEM] * chunks,
        out_shape=[shape((sides, rows // ring, width))] * chunks,
        compiler_params=grant(),
        cost_estimate=cost(own.size, 6 * own.size),
        name="fold",
    )(first, own, mate)


def rows_dot(left, right):
    return lax.dot_general(
        left, right, (((0,), (0,)), ((), ())), preferred_element_type=F32
    ).astype(BF)


def on_device(tokens, modality, gate, up, down, out_grad):
    _, width = out_grad.shape
    groups = lax.axis_size("seq")
    ring = lax.axis_size("dp") // CORES
    part = width // groups
    seat = lax.axis_index("seq").reshape(1)
    first = (lax.axis_index("dp") < CORES).astype(jnp.int32).reshape(1)
    tokens, modality, first, seat = lax.optimization_barrier((tokens, modality, first, seat))

    def shift(value, k):
        return lax.ppermute(value, "dp", [
            (z * CORES + c, (z + k) % ring * CORES + c) for z in range(ring) for c in range(CORES)])

    def swap(value):
        return lax.ppermute(value, "dp", [
            (z * CORES + c, z * CORES + 1 - c) for z in range(ring) for c in range(CORES)])

    def across(value, mask):
        return lax.ppermute(value, "seq", [(g, g ^ mask) for g in range(groups)])

    def gathered(block):
        return jnp.concatenate([block] + [shift(block, k) for k in range(1, ring)], axis=0)

    def slices_of(blocks):
        small = jnp.stack([blocks[0]] + [across(blocks[m], m) for m in range(1, groups)])
        pieces = [small] + [shift(small, k) for k in range(1, ring)]
        own = jnp.stack(pieces, axis=1)
        mate = swap(own)
        both_cores = jnp.stack([own, mate], axis=1)
        return (both_cores[..., :part].reshape(-1, part), both_cores[..., part:].reshape(-1, part))

    def near(value):
        held = [[value]] + [None] * (groups - 1)
        for m in range(1, groups):
            if m & (m - 1) == 0:
                held[m] = [across(value, m)]
        return held

    def relay(held):
        held = list(held)
        for m in range(1, groups):
            low, high = m & -m, 1 << (m.bit_length() - 1)
            if low != high:
                held[m] = [across(held[m ^ low][0], low), across(held[m ^ high][1], high)]
        return held

    def after(values, others):
        leaves, tree = jax.tree.flatten(values)
        return jax.tree.unflatten(
            tree, lax.optimization_barrier((*leaves, *others))[:len(leaves)])

    def returned(own, mate):
        line = ring == 4
        sums = fold(first, own, mate, ring, ring + line)
        if not line:
            return [sums[0]] + [shift(sums[k], -k) for k in range(1, ring)], sums[0]

        def along(value, pairs):
            return lax.ppermute(value, "dp", [
                (a * CORES + c, b * CORES + c) for a, b in pairs for c in range(CORES)])

        far = along(sums[4], [(0, 1), (3, 2)])
        terms = [along(sums[1], [(1, 0), (2, 1), (3, 2)]),
                 along(sums[3], [(0, 1), (1, 2), (2, 3)])]
        mid = (sums[2].astype(F32) + far.astype(F32)).astype(BF)
        return [sums[0], *terms, shift(mid, 2)], mid

    def stack(held):
        return jnp.concatenate(sum(held, []), axis=0)

    left, right, *blocks = pick(seat, modality, tokens, out_grad, groups)
    tok = [gathered(side) for side in (left, right)]
    tok_mate = []
    for side in tok:
        tok_mate.append(swap(side))
    tok_all, cot_all = slices_of(blocks)
    cot = gathered(out_grad)
    cot_mate = swap(cot)
    before = enter(tok[0], tok_mate[0], gate, up)
    hid, active, factor = enter(tok[1], tok_mate[1], gate, up, *before)
    rows = hid.shape[0]
    all_hid = near(hid)
    all_hid = [v and [v[0][:rows // 2], v[0][rows // 2:]] for v in all_hid]
    all_hid = relay(all_hid)
    both = turn(cot, cot_mate, down, active, factor)
    all_both = near(both)
    own, other = leave(hid, both, gate, up, down)

    mate = swap(other)
    terms, last = returned(own, mate)
    all_hid = after(all_hid, [last])
    all_both = after(all_both, [last])
    all_gb, all_ub = ([v and [v[0][side, :rows // 2], v[0][side, rows // 2:]] for v in all_both]
                      for side in range(2))
    all_gb = relay(all_gb)
    all_ub = relay(all_ub)
    down_grad = rows_dot(stack(all_hid), cot_all)
    gate_grad = rows_dot(tok_all, stack(all_gb))
    up_grad = rows_dot(tok_all, stack(all_ub))
    terms = after(terms, [up_grad])

    def total(side):
        value = terms[0][side].astype(F32)
        for term in terms[1:]:
            value = value + term[side].astype(F32)
        return value.astype(BF)

    output, in_grad = total(0), total(1)
    return output, in_grad, gate_grad, up_grad, down_grad


def solution(mesh):
    rows = P(("dp", "seq"), None)
    return jax.shard_map(
        on_device,
        mesh=mesh,
        in_specs=(rows, P(("dp", "seq")), P(None, "dp"), P(None, "dp"), P("dp", None), rows),
        out_specs=(rows, rows, P("seq", "dp"), P("seq", "dp"), P("dp", "seq")),
        check_vma=False,
    )
```

```python
import jax
import jax.numpy as jnp
from jax import lax
from jax.experimental import pallas as pl
from jax.experimental.pallas import tpu as pltpu
from jax.sharding import PartitionSpec as P


BF = jnp.bfloat16
F32 = jnp.float32
CORES = 2
MIB = 1 << 20
ALL_VMEM = 67043328


HBM = pl.BlockSpec(memory_space=pltpu.HBM)
VMEM = pl.BlockSpec(memory_space=pltpu.VMEM)


def tile_of(extent, options):
    for option in options:
        if extent % option == 0:
            return option
    return extent


def cost(flops, nbytes):
    return pl.CostEstimate(flops=flops, bytes_accessed=nbytes, transcendentals=0)


def shape(dims, dtype=BF):
    return jax.ShapeDtypeStruct(dims, dtype)


def grant(*arrays, least=0):
    total = sum(2 * r * c if d == BF else 4 * r * c for r, c, d in arrays)
    return pltpu.CompilerParams(vmem_limit_bytes=min(max(total + 6 * MIB, least), ALL_VMEM))


def nt_dot(left, right):
    return lax.dot_general(left, right, (((1,), (1,)), ((), ())), preferred_element_type=F32)


def nn_dot(left, right):
    return jnp.dot(left, right, preferred_element_type=F32)


def pick_kernel(seat_ref, flag_ref, tokens_ref, cot_ref, left_ref, right_ref, *refs):
    blocks, picked_ref = refs[:-1], refs[-1]
    rows = cot_ref.shape[0]
    count = tokens_ref.shape[0]
    flags = (flag_ref[...] == 1).astype(F32)
    before = lax.broadcasted_iota(jnp.int32, (count, count), 0)
    after = lax.broadcasted_iota(jnp.int32, (count, count), 1)
    ranks = nn_dot(flags, (before <= after).astype(F32))
    slots = lax.broadcasted_iota(jnp.int32, (rows, count), 0).astype(F32) + 1.0
    chosen = (jnp.broadcast_to(ranks, (rows, count)) == slots) & (
        jnp.broadcast_to(flags, (rows, count)) == 1.0
    )
    picked_ref[...] = nn_dot(chosen.astype(BF), tokens_ref[...]).astype(BF)
    middle = left_ref.shape[1]
    left_ref[...] = picked_ref[:, :middle]
    right_ref[...] = picked_ref[:, middle:]
    part = picked_ref.shape[1] // len(blocks)
    for m, block in enumerate(blocks):
        span = pl.ds(pl.multiple_of((seat_ref[0] ^ m) * part, part), part)
        block[:, :part] = picked_ref[:, span]
        block[:, part:] = cot_ref[:, span]


def pick(seat, modality, tokens, out_grad, groups):
    rows, width = out_grad.shape
    half, block = shape((rows, width // 2)), shape((rows, 2 * width // groups))
    return pl.pallas_call(
        pick_kernel,
        in_specs=[pl.BlockSpec(memory_space=pltpu.SMEM)] + [VMEM] * 3,
        out_specs=[VMEM] * (2 + groups),
        out_shape=[half, half] + [block] * groups,
        scratch_shapes=[pltpu.VMEM((rows, width), BF)],
        compiler_params=grant(),
        name="pick",
    )(seat, modality.reshape(1, -1), tokens, out_grad)


def streamed(steps, depth, copies, body, first):
    depth = min(depth, steps)

    def start(j):
        for copy in copies(j, lax.rem(j, depth)):
            copy.start()

    for j in range(depth):
        start(jnp.int32(j))
    first()

    @pl.loop(0, steps)
    def _(j):
        slot = lax.rem(j, depth)
        for copy in copies(j, slot):
            copy.wait()
        body(j, slot)

        @pl.when(j + depth < steps)
        def _():
            start(j + depth)


DEPTH = 5


def enter_kernel(tile, last, xa_ref, xb_ref, gate_hbm, up_hbm, *refs):
    (*before, hid_ref, active_ref, turn_ref) = refs[:5] if last else (None, *refs[:2])
    x_ref, gate_ref, up_ref, sems = refs[5:] if last else refs[2:]
    half, depth = xa_ref.shape
    rows = pl.ds(depth if last else 0, depth)

    def first():
        x_ref[:half] = xa_ref[...]
        x_ref[half:] = xb_ref[...]

    def copies(j, slot):
        column = pl.ds(pl.multiple_of(j * tile, tile), tile)
        return (
            pltpu.make_async_copy(gate_hbm.at[rows, column], gate_ref.at[slot], sems.at[0, slot]),
            pltpu.make_async_copy(up_hbm.at[rows, column], up_ref.at[slot], sems.at[1, slot]),
        )

    def body(j, slot):
        column = pl.ds(pl.multiple_of(j * tile, tile), tile)
        gate_proj = nn_dot(x_ref[...], gate_ref[slot])
        up_proj = nn_dot(x_ref[...], up_ref[slot])
        if not last:
            active_ref[:, column] = gate_proj
            turn_ref[:, column] = up_proj
            return
        gate_proj = gate_proj + before[0][:, column]
        up_proj = up_proj + before[1][:, column]
        sig = jax.nn.sigmoid(gate_proj)
        active = gate_proj * sig
        hid_ref[:, column] = (active * up_proj).astype(BF)
        active_ref[:, column] = active
        turn_ref[:, column] = up_proj * (sig * (1.0 + gate_proj * (1.0 - sig)))

    streamed(gate_hbm.shape[1] // tile, gate_ref.shape[0], copies, body, first)


def enter(own, other, gate, up, *before):
    half, width = own.shape
    units = gate.shape[1]
    rows = 2 * half
    tile = tile_of(units, (256, 128))
    depth = min(DEPTH, units // tile)
    last = len(before) > 0
    wide = shape((rows, units), F32)
    outs = [shape((rows, units)), wide, wide] if last else [wide, wide]
    return pl.pallas_call(
        lambda *refs: enter_kernel(tile, last, *refs),
        in_specs=[VMEM, VMEM, HBM, HBM] + [VMEM] * len(before),
        out_specs=[VMEM] * len(outs),
        out_shape=outs,
        scratch_shapes=[
            pltpu.VMEM((rows, width), BF),
            pltpu.VMEM((depth, width, tile), BF),
            pltpu.VMEM((depth, width, tile), BF),
            pltpu.SemaphoreType.DMA((2, depth)),
        ],
        compiler_params=grant((rows, width, BF), (2 * depth * tile, width, BF), least=46 * MIB),
        cost_estimate=cost(4 * rows * width * units, 4 * width * units),
        name="enter",
    )(own, other, gate, up, *before)


def turn_kernel(tile, ca_ref, cb_ref, down_hbm, active_ref, factor_ref, both_ref,
                c_ref, down_ref, sems):
    half = ca_ref.shape[0]

    def first():
        c_ref[:half] = ca_ref[...]
        c_ref[half:] = cb_ref[...]

    def copies(j, slot):
        row = pl.ds(pl.multiple_of(j * tile, tile), tile)
        return (pltpu.make_async_copy(down_hbm.at[row, :], down_ref.at[slot], sems.at[slot]),)

    def body(j, slot):
        span = pl.ds(pl.multiple_of(j * tile, tile), tile)
        back = nt_dot(c_ref[...], down_ref[slot])
        both_ref[0, :, span] = (back * factor_ref[:, span]).astype(BF)
        both_ref[1, :, span] = (back * active_ref[:, span]).astype(BF)

    streamed(down_hbm.shape[0] // tile, down_ref.shape[0], copies, body, first)


def turn(own, other, down, active, factor):
    half, width = own.shape
    units = down.shape[0]
    rows = 2 * half
    tile = tile_of(units, (256, 128))
    depth = min(DEPTH, units // tile)
    return pl.pallas_call(
        lambda *refs: turn_kernel(tile, *refs),
        in_specs=[VMEM, VMEM, HBM, VMEM, VMEM],
        out_specs=VMEM,
        out_shape=shape((2, rows, units)),
        scratch_shapes=[
            pltpu.VMEM((rows, width), BF),
            pltpu.VMEM((depth, tile, width), BF),
            pltpu.SemaphoreType.DMA((depth,)),
        ],
        compiler_params=grant((rows, width, BF), (depth * tile, width, BF), least=46 * MIB),
        cost_estimate=cost(2 * rows * width * units, 2 * width * units),
        name="turn",
    )(own, other, down, active, factor)


def leave_kernel(step, hid_ref, both_ref, gate_hbm, up_hbm, down_hbm, own_ref, other_ref,
                 gate_ref, up_ref, down_ref, sems):
    half = own_ref.shape[1]

    def copies(j, slot):
        span = pl.ds(pl.multiple_of(j * step, step), step)
        return (
            pltpu.make_async_copy(down_hbm.at[:, span], down_ref.at[slot], sems.at[0, slot]),
            pltpu.make_async_copy(gate_hbm.at[span, :], gate_ref.at[slot], sems.at[1, slot]),
            pltpu.make_async_copy(up_hbm.at[span, :], up_ref.at[slot], sems.at[2, slot]),
        )

    def body(j, slot):
        span = pl.ds(pl.multiple_of(j * step, step), step)
        result = nn_dot(hid_ref[...], down_ref[slot]).astype(BF)
        own_ref[0, :, span] = result[:half]
        other_ref[0, :, span] = result[half:]
        result = nt_dot(both_ref[0], gate_ref[slot]) + nt_dot(both_ref[1], up_ref[slot])
        result = result.astype(BF)
        own_ref[1, :, span] = result[:half]
        other_ref[1, :, span] = result[half:]

    streamed(gate_hbm.shape[0] // step, gate_ref.shape[0], copies, body, lambda: None)


def leave(hid, both, gate, up, down):
    rows, units = hid.shape
    width = gate.shape[0]
    half = rows // 2
    step = tile_of(width, (512, 256, 128))
    depth = min(DEPTH, width // step)
    return pl.pallas_call(
        lambda *refs: leave_kernel(step, *refs),
        in_specs=[VMEM] * 2 + [HBM] * 3,
        out_specs=[VMEM] * 2,
        out_shape=[shape((2, half, width))] * 2,
        scratch_shapes=[
            pltpu.VMEM((depth, step, units), BF),
            pltpu.VMEM((depth, step, units), BF),
            pltpu.VMEM((depth, units, step), BF),
            pltpu.SemaphoreType.DMA((3, depth)),
        ],
        compiler_params=grant((3 * depth * step, units, BF), least=40 * MIB),
        cost_estimate=cost(6 * rows * width * units, 6 * width * units),
        name="leave",
    )(hid, both, gate, up, down)


def fold_kernel(first_ref, own_ref, mate_ref, *chunks):
    count = chunks[0].shape[1]
    ring = own_ref.shape[1] // count
    for k in range(ring):
        span = slice(k * count, (k + 1) * count)
        both = own_ref[:, span].astype(F32) + mate_ref[:, span].astype(F32)
        chunks[k][...] = both.astype(BF)
    if len(chunks) > ring:
        @pl.when(first_ref[0] == 1)
        def _():
            chunks[ring][...] = chunks[1][...]

        @pl.when(first_ref[0] != 1)
        def _():
            chunks[ring][...] = chunks[ring - 1][...]


def fold(first, own, mate, ring, chunks):
    sides, rows, width = own.shape
    return pl.pallas_call(
        fold_kernel,
        in_specs=[pl.BlockSpec(memory_space=pltpu.SMEM), VMEM, VMEM],
        out_specs=[VMEM] * chunks,
        out_shape=[shape((sides, rows // ring, width))] * chunks,
        compiler_params=grant(),
        cost_estimate=cost(own.size, 6 * own.size),
        name="fold",
    )(first, own, mate)


def sums_dot(left, right):
    return lax.dot_general(left, right, (((0,), (0,)), ((), ())), preferred_element_type=F32)


def rows_dot(left, right):
    return sums_dot(left, right).astype(BF)


def on_device(tokens, modality, gate, up, down, out_grad):
    _, width = out_grad.shape
    groups = lax.axis_size("seq")
    ring = lax.axis_size("dp") // CORES
    part = width // groups
    seat = lax.axis_index("seq").reshape(1)
    first = (lax.axis_index("dp") < CORES).astype(jnp.int32).reshape(1)
    tokens, modality, first, seat = lax.optimization_barrier((tokens, modality, first, seat))

    def shift(value, k):
        return lax.ppermute(value, "dp", [
            (z * CORES + c, (z + k) % ring * CORES + c) for z in range(ring) for c in range(CORES)])

    def swap(value):
        return lax.ppermute(value, "dp", [
            (z * CORES + c, z * CORES + 1 - c) for z in range(ring) for c in range(CORES)])

    def across(value, mask):
        return lax.ppermute(value, "seq", [(g, g ^ mask) for g in range(groups)])

    def gathered(block):
        return jnp.concatenate([block] + [shift(block, k) for k in range(1, ring)], axis=0)

    def slices_of(blocks):
        small = jnp.stack([blocks[0]] + [across(blocks[m], m) for m in range(1, groups)])
        pieces = [small] + [shift(small, k) for k in range(1, ring)]
        own = jnp.stack(pieces, axis=1)
        mate = swap(own)
        both_cores = jnp.stack([own, mate], axis=1)
        return (both_cores[..., :part].reshape(-1, part), both_cores[..., part:].reshape(-1, part))

    def near(value):
        held = [[value]] + [None] * (groups - 1)
        for m in range(1, groups):
            if m & (m - 1) == 0:
                held[m] = [across(value, m)]
        return held

    def relay(held):
        held = list(held)
        for m in range(1, groups):
            low, high = m & -m, 1 << (m.bit_length() - 1)
            if low != high:
                held[m] = [across(held[m ^ low][0], low), across(held[m ^ high][1], high)]
        return held

    def after(values, others):
        leaves, tree = jax.tree.flatten(values)
        return jax.tree.unflatten(
            tree, lax.optimization_barrier((*leaves, *others))[:len(leaves)])

    def returned(own, mate):
        line = ring == 4
        sums = fold(first, own, mate, ring, ring + line)
        if not line:
            return [sums[0]] + [shift(sums[k], -k) for k in range(1, ring)], sums[0]

        def along(value, pairs):
            return lax.ppermute(value, "dp", [
                (a * CORES + c, b * CORES + c) for a, b in pairs for c in range(CORES)])

        far = along(sums[4], [(0, 1), (3, 2)])
        terms = [along(sums[1], [(1, 0), (2, 1), (3, 2)]),
                 along(sums[3], [(0, 1), (1, 2), (2, 3)])]
        mid = (sums[2].astype(F32) + far.astype(F32)).astype(BF)
        return [sums[0], *terms, shift(mid, 2)], mid

    def stack(held):
        return jnp.concatenate(sum(held, []), axis=0)

    left, right, *blocks = pick(seat, modality, tokens, out_grad, groups)
    tok = [gathered(side) for side in (left, right)]
    tok_mate = []
    for side in tok:
        tok_mate.append(swap(side))
    tok_all, cot_all = slices_of(blocks)
    cot = gathered(out_grad)
    cot_mate = swap(cot)
    before = enter(tok[0], tok_mate[0], gate, up)
    hid, active, factor = enter(tok[1], tok_mate[1], gate, up, *before)
    rows = hid.shape[0]
    all_hid = near(hid)
    all_hid = [v and [v[0][:rows // 2], v[0][rows // 2:]] for v in all_hid]
    all_hid = relay(all_hid)
    both = turn(cot, cot_mate, down, active, factor)
    all_both = near(both)
    own, other = leave(hid, both, gate, up, down)

    mate = swap(other)
    terms, last = returned(own, mate)
    all_hid = after(all_hid, [last])
    all_both = after(all_both, [last])
    all_gb, all_ub = ([v and [v[0][side, :rows // 2], v[0][side, rows // 2:]] for v in all_both]
                      for side in range(2))
    all_gb = relay(all_gb)
    all_ub = relay(all_ub)
    down_grad = rows_dot(stack(all_hid), cot_all)
    gate_grad = rows_dot(tok_all, stack(all_gb))
    up_grad = sums_dot(tok_all[:-rows], stack(all_ub[:-1]))
    up_grad = (up_grad + sums_dot(tok_all[-rows:], stack(all_ub[-1:]))).astype(BF)
    terms = after(terms, [up_grad])

    def total(side):
        value = terms[0][side].astype(F32)
        for term in terms[1:]:
            value = value + term[side].astype(F32)
        return value.astype(BF)

    output, in_grad = total(0), total(1)
    return output, in_grad, gate_grad, up_grad, down_grad


def solution(mesh):
    rows = P(("dp", "seq"), None)
    return jax.shard_map(
        on_device,
        mesh=mesh,
        in_specs=(rows, P(("dp", "seq")), P(None, "dp"), P(None, "dp"), P("dp", None), rows),
        out_specs=(rows, rows, P("seq", "dp"), P("seq", "dp"), P("dp", "seq")),
        check_vma=False,
    )
```

```python
import jax
import jax.numpy as jnp
from jax import lax
from jax.experimental import pallas as pl
from jax.experimental.pallas import tpu as pltpu
from jax.sharding import PartitionSpec as P


BF = jnp.bfloat16
F32 = jnp.float32
CORES = 2
MIB = 1 << 20
ALL_VMEM = 67043328


HBM = pl.BlockSpec(memory_space=pltpu.HBM)
VMEM = pl.BlockSpec(memory_space=pltpu.VMEM)


def tile_of(extent, options):
    for option in options:
        if extent % option == 0:
            return option
    return extent


def cost(flops, nbytes):
    return pl.CostEstimate(flops=flops, bytes_accessed=nbytes, transcendentals=0)


def shape(dims, dtype=BF):
    return jax.ShapeDtypeStruct(dims, dtype)


def grant(*arrays, least=0):
    total = sum(2 * r * c if d == BF else 4 * r * c for r, c, d in arrays)
    return pltpu.CompilerParams(vmem_limit_bytes=min(max(total + 6 * MIB, least), ALL_VMEM))


def nt_dot(left, right):
    return lax.dot_general(left, right, (((1,), (1,)), ((), ())), preferred_element_type=F32)


def nn_dot(left, right):
    return jnp.dot(left, right, preferred_element_type=F32)


def pick_kernel(flag_ref, tokens_ref, picked_ref, left_ref, right_ref):
    rows = picked_ref.shape[0]
    count = tokens_ref.shape[0]
    flags = (flag_ref[...] == 1).astype(F32)
    before = lax.broadcasted_iota(jnp.int32, (count, count), 0)
    after = lax.broadcasted_iota(jnp.int32, (count, count), 1)
    ranks = nn_dot(flags, (before <= after).astype(F32))
    slots = lax.broadcasted_iota(jnp.int32, (rows, count), 0).astype(F32) + 1.0
    chosen = (jnp.broadcast_to(ranks, (rows, count)) == slots) & (
        jnp.broadcast_to(flags, (rows, count)) == 1.0
    )
    picked_ref[...] = nn_dot(chosen.astype(BF), tokens_ref[...]).astype(BF)
    middle = left_ref.shape[1]
    left_ref[...] = picked_ref[:, :middle]
    right_ref[...] = picked_ref[:, middle:]


def pick(modality, tokens, rows):
    width = tokens.shape[1]
    half = shape((rows, width // 2))
    return pl.pallas_call(
        pick_kernel,
        in_specs=[VMEM] * 2,
        out_specs=[VMEM] * 3,
        out_shape=[shape((rows, width)), half, half],
        compiler_params=grant(),
        name="pick",
    )(modality.reshape(1, -1), tokens)


def cut_kernel(seat_ref, picked_ref, cot_ref, *blocks):
    part = picked_ref.shape[1] // len(blocks)
    for m, block in enumerate(blocks):
        span = pl.ds(pl.multiple_of((seat_ref[0] ^ m) * part, part), part)
        block[:, :part] = picked_ref[:, span]
        block[:, part:] = cot_ref[:, span]


def cut(seat, picked, out_grad, groups):
    rows, width = out_grad.shape
    return pl.pallas_call(
        cut_kernel,
        in_specs=[pl.BlockSpec(memory_space=pltpu.SMEM)] + [VMEM] * 2,
        out_specs=[VMEM] * groups,
        out_shape=[shape((rows, 2 * width // groups))] * groups,
        compiler_params=grant(),
        name="cut",
    )(seat, picked, out_grad)


def streamed(steps, depth, copies, body, first):
    depth = min(depth, steps)

    def start(j):
        for copy in copies(j, lax.rem(j, depth)):
            copy.start()

    for j in range(depth):
        start(jnp.int32(j))
    first()

    @pl.loop(0, steps)
    def _(j):
        slot = lax.rem(j, depth)
        for copy in copies(j, slot):
            copy.wait()
        body(j, slot)

        @pl.when(j + depth < steps)
        def _():
            start(j + depth)


DEPTH = 5


def enter_kernel(tile, last, xa_ref, xb_ref, gate_hbm, up_hbm, *refs):
    (*before, hid_ref, active_ref, turn_ref) = refs[:5] if last else (None, *refs[:2])
    x_ref, gate_ref, up_ref, sems = refs[5:] if last else refs[2:]
    half, depth = xa_ref.shape
    rows = pl.ds(depth if last else 0, depth)

    def first():
        x_ref[:half] = xa_ref[...]
        x_ref[half:] = xb_ref[...]

    def copies(j, slot):
        column = pl.ds(pl.multiple_of(j * tile, tile), tile)
        return (
            pltpu.make_async_copy(gate_hbm.at[rows, column], gate_ref.at[slot], sems.at[0, slot]),
            pltpu.make_async_copy(up_hbm.at[rows, column], up_ref.at[slot], sems.at[1, slot]),
        )

    def body(j, slot):
        column = pl.ds(pl.multiple_of(j * tile, tile), tile)
        gate_proj = nn_dot(x_ref[...], gate_ref[slot])
        up_proj = nn_dot(x_ref[...], up_ref[slot])
        if not last:
            active_ref[:, column] = gate_proj
            turn_ref[:, column] = up_proj
            return
        gate_proj = gate_proj + before[0][:, column]
        up_proj = up_proj + before[1][:, column]
        sig = jax.nn.sigmoid(gate_proj)
        active = gate_proj * sig
        hid_ref[:, column] = (active * up_proj).astype(BF)
        active_ref[:, column] = active
        turn_ref[:, column] = up_proj * (sig * (1.0 + gate_proj * (1.0 - sig)))

    streamed(gate_hbm.shape[1] // tile, gate_ref.shape[0], copies, body, first)


def enter(own, other, gate, up, *before):
    half, width = own.shape
    units = gate.shape[1]
    rows = 2 * half
    tile = tile_of(units, (256, 128))
    depth = min(DEPTH, units // tile)
    last = len(before) > 0
    wide = shape((rows, units), F32)
    outs = [shape((rows, units)), wide, wide] if last else [wide, wide]
    return pl.pallas_call(
        lambda *refs: enter_kernel(tile, last, *refs),
        in_specs=[VMEM, VMEM, HBM, HBM] + [VMEM] * len(before),
        out_specs=[VMEM] * len(outs),
        out_shape=outs,
        scratch_shapes=[
            pltpu.VMEM((rows, width), BF),
            pltpu.VMEM((depth, width, tile), BF),
            pltpu.VMEM((depth, width, tile), BF),
            pltpu.SemaphoreType.DMA((2, depth)),
        ],
        compiler_params=grant((rows, width, BF), (2 * depth * tile, width, BF), least=46 * MIB),
        cost_estimate=cost(4 * rows * width * units, 4 * width * units),
        name="enter",
    )(own, other, gate, up, *before)


def turn_kernel(tile, ca_ref, cb_ref, down_hbm, active_ref, factor_ref, both_ref,
                c_ref, down_ref, sems):
    half = ca_ref.shape[0]

    def first():
        c_ref[:half] = ca_ref[...]
        c_ref[half:] = cb_ref[...]

    def copies(j, slot):
        row = pl.ds(pl.multiple_of(j * tile, tile), tile)
        return (pltpu.make_async_copy(down_hbm.at[row, :], down_ref.at[slot], sems.at[slot]),)

    def body(j, slot):
        span = pl.ds(pl.multiple_of(j * tile, tile), tile)
        back = nt_dot(c_ref[...], down_ref[slot])
        both_ref[0, :, span] = (back * factor_ref[:, span]).astype(BF)
        both_ref[1, :, span] = (back * active_ref[:, span]).astype(BF)

    streamed(down_hbm.shape[0] // tile, down_ref.shape[0], copies, body, first)


def turn(own, other, down, active, factor):
    half, width = own.shape
    units = down.shape[0]
    rows = 2 * half
    tile = tile_of(units, (256, 128))
    depth = min(DEPTH, units // tile)
    return pl.pallas_call(
        lambda *refs: turn_kernel(tile, *refs),
        in_specs=[VMEM, VMEM, HBM, VMEM, VMEM],
        out_specs=VMEM,
        out_shape=shape((2, rows, units)),
        scratch_shapes=[
            pltpu.VMEM((rows, width), BF),
            pltpu.VMEM((depth, tile, width), BF),
            pltpu.SemaphoreType.DMA((depth,)),
        ],
        compiler_params=grant((rows, width, BF), (depth * tile, width, BF), least=46 * MIB),
        cost_estimate=cost(2 * rows * width * units, 2 * width * units),
        name="turn",
    )(own, other, down, active, factor)


def leave_kernel(step, hid_ref, both_ref, gate_hbm, up_hbm, down_hbm, own_ref, other_ref,
                 gate_ref, up_ref, down_ref, sems):
    half = own_ref.shape[1]

    def copies(j, slot):
        span = pl.ds(pl.multiple_of(j * step, step), step)
        return (
            pltpu.make_async_copy(down_hbm.at[:, span], down_ref.at[slot], sems.at[0, slot]),
            pltpu.make_async_copy(gate_hbm.at[span, :], gate_ref.at[slot], sems.at[1, slot]),
            pltpu.make_async_copy(up_hbm.at[span, :], up_ref.at[slot], sems.at[2, slot]),
        )

    def body(j, slot):
        span = pl.ds(pl.multiple_of(j * step, step), step)
        result = nn_dot(hid_ref[...], down_ref[slot]).astype(BF)
        own_ref[0, :, span] = result[:half]
        other_ref[0, :, span] = result[half:]
        result = nt_dot(both_ref[0], gate_ref[slot]) + nt_dot(both_ref[1], up_ref[slot])
        result = result.astype(BF)
        own_ref[1, :, span] = result[:half]
        other_ref[1, :, span] = result[half:]

    streamed(gate_hbm.shape[0] // step, gate_ref.shape[0], copies, body, lambda: None)


def leave(hid, both, gate, up, down):
    rows, units = hid.shape
    width = gate.shape[0]
    half = rows // 2
    step = tile_of(width, (512, 256, 128))
    depth = min(DEPTH, width // step)
    return pl.pallas_call(
        lambda *refs: leave_kernel(step, *refs),
        in_specs=[VMEM] * 2 + [HBM] * 3,
        out_specs=[VMEM] * 2,
        out_shape=[shape((2, half, width))] * 2,
        scratch_shapes=[
            pltpu.VMEM((depth, step, units), BF),
            pltpu.VMEM((depth, step, units), BF),
            pltpu.VMEM((depth, units, step), BF),
            pltpu.SemaphoreType.DMA((3, depth)),
        ],
        compiler_params=grant((3 * depth * step, units, BF), least=40 * MIB),
        cost_estimate=cost(6 * rows * width * units, 6 * width * units),
        name="leave",
    )(hid, both, gate, up, down)


def fold_kernel(first_ref, own_ref, mate_ref, *chunks):
    count = chunks[0].shape[1]
    ring = own_ref.shape[1] // count
    for k in range(ring):
        span = slice(k * count, (k + 1) * count)
        both = own_ref[:, span].astype(F32) + mate_ref[:, span].astype(F32)
        chunks[k][...] = both.astype(BF)
    if len(chunks) > ring:
        @pl.when(first_ref[0] == 1)
        def _():
            chunks[ring][...] = chunks[1][...]

        @pl.when(first_ref[0] != 1)
        def _():
            chunks[ring][...] = chunks[ring - 1][...]


def fold(first, own, mate, ring, chunks):
    sides, rows, width = own.shape
    return pl.pallas_call(
        fold_kernel,
        in_specs=[pl.BlockSpec(memory_space=pltpu.SMEM), VMEM, VMEM],
        out_specs=[VMEM] * chunks,
        out_shape=[shape((sides, rows // ring, width))] * chunks,
        compiler_params=grant(),
        cost_estimate=cost(own.size, 6 * own.size),
        name="fold",
    )(first, own, mate)


def sums_dot(left, right):
    return lax.dot_general(left, right, (((0,), (0,)), ((), ())), preferred_element_type=F32)


def rows_dot(left, right):
    return sums_dot(left, right).astype(BF)


def on_device(tokens, modality, gate, up, down, out_grad):
    count, width = out_grad.shape
    groups = lax.axis_size("seq")
    ring = lax.axis_size("dp") // CORES
    part = width // groups
    seat = lax.axis_index("seq").reshape(1)
    first = (lax.axis_index("dp") < CORES).astype(jnp.int32).reshape(1)
    tokens, modality, first, seat = lax.optimization_barrier((tokens, modality, first, seat))

    def shift(value, k):
        return lax.ppermute(value, "dp", [
            (z * CORES + c, (z + k) % ring * CORES + c) for z in range(ring) for c in range(CORES)])

    def swap(value):
        return lax.ppermute(value, "dp", [
            (z * CORES + c, z * CORES + 1 - c) for z in range(ring) for c in range(CORES)])

    def across(value, mask):
        return lax.ppermute(value, "seq", [(g, g ^ mask) for g in range(groups)])

    def gathered(block):
        return jnp.concatenate([block] + [shift(block, k) for k in range(1, ring)], axis=0)

    def slices_of(blocks):
        small = jnp.stack([blocks[0]] + [across(blocks[m], m) for m in range(1, groups)])
        pieces = [small] + [shift(small, k) for k in range(1, ring)]
        own = jnp.stack(pieces, axis=1)
        mate = swap(own)
        both_cores = jnp.stack([own, mate], axis=1)
        return (both_cores[..., :part].reshape(-1, part), both_cores[..., part:].reshape(-1, part))

    def near(value):
        held = [[value]] + [None] * (groups - 1)
        for m in range(1, groups):
            if m & (m - 1) == 0:
                held[m] = [across(value, m)]
        return held

    def relay(held):
        held = list(held)
        for m in range(1, groups):
            low, high = m & -m, 1 << (m.bit_length() - 1)
            if low != high:
                held[m] = [across(held[m ^ low][0], low), across(held[m ^ high][1], high)]
        return held

    def after(values, others):
        leaves, tree = jax.tree.flatten(values)
        return jax.tree.unflatten(
            tree, lax.optimization_barrier((*leaves, *others))[:len(leaves)])

    def returned(own, mate):
        line = ring == 4
        sums = fold(first, own, mate, ring, ring + line)
        if not line:
            return [sums[0]] + [shift(sums[k], -k) for k in range(1, ring)], sums[0]

        def along(value, pairs):
            return lax.ppermute(value, "dp", [
                (a * CORES + c, b * CORES + c) for a, b in pairs for c in range(CORES)])

        far = along(sums[4], [(0, 1), (3, 2)])
        terms = [along(sums[1], [(1, 0), (2, 1), (3, 2)]),
                 along(sums[3], [(0, 1), (1, 2), (2, 3)])]
        mid = (sums[2].astype(F32) + far.astype(F32)).astype(BF)
        return [sums[0], *terms, shift(mid, 2)], mid

    def stack(held):
        return jnp.concatenate(sum(held, []), axis=0)

    picked, left, right = pick(modality, tokens, count)
    blocks = cut(seat, picked, out_grad, groups)
    tok = [gathered(side) for side in (left, right)]
    tok_mate = []
    for side in tok:
        tok_mate.append(swap(side))
    tok_all, cot_all = slices_of(blocks)
    cot = gathered(out_grad)
    cot_mate = swap(cot)
    before = enter(tok[0], tok_mate[0], gate, up)
    hid, active, factor = enter(tok[1], tok_mate[1], gate, up, *before)
    rows = hid.shape[0]
    all_hid = near(hid)
    all_hid = [v and [v[0][:rows // 2], v[0][rows // 2:]] for v in all_hid]
    all_hid = relay(all_hid)
    both = turn(cot, cot_mate, down, active, factor)
    all_both = near(both)
    own, other = leave(hid, both, gate, up, down)

    mate = swap(other)
    terms, last = returned(own, mate)
    all_both = after(all_both, [last])
    all_gb, all_ub = ([v and [v[0][side, :rows // 2], v[0][side, rows // 2:]] for v in all_both]
                      for side in range(2))
    all_gb = relay(all_gb)
    all_ub = relay(all_ub)
    up_grad = sums_dot(tok_all[:-rows], stack(all_ub[:-1]))
    all_hid = after(all_hid, [up_grad])
    down_grad = rows_dot(stack(all_hid), cot_all)
    gate_grad = rows_dot(tok_all, stack(all_gb))
    up_grad = (up_grad + sums_dot(tok_all[-rows:], stack(all_ub[-1:]))).astype(BF)
    terms = after(terms, [up_grad])

    def total(side):
        value = terms[0][side].astype(F32)
        for term in terms[1:]:
            value = value + term[side].astype(F32)
        return value.astype(BF)

    output, in_grad = total(0), total(1)
    return output, in_grad, gate_grad, up_grad, down_grad


def solution(mesh):
    rows = P(("dp", "seq"), None)
    return jax.shard_map(
        on_device,
        mesh=mesh,
        in_specs=(rows, P(("dp", "seq")), P(None, "dp"), P(None, "dp"), P("dp", None), rows),
        out_specs=(rows, rows, P("seq", "dp"), P("seq", "dp"), P("dp", "seq")),
        check_vma=False,
    )
```
